1024 devices in a mesh: seq: 32 (over y, x_hi, core), head: 32 (over z, x_lo).
Axes of the slice: x: 8 (x_hi: 2, x_lo: 4; x = x_hi * 4 + x_lo), y: 8, z: 8, core: 2. Of those that a mesh axis runs over, the one named last changes fastest.
Arguments:
- main_query: bfloat16 [4096, 73728], P('seq', 'head'), may hold values from -18 to 18
- latent: bfloat16 [8192, 576], P('seq'), may hold values from -6 to 6
- main_outside: float32 [4096, 128], P('seq', 'head'), may hold values from 5 to 11
- index_query: bfloat16 [4096, 8192], P('seq', 'head'), may hold values from -6 to 6
- index_weights: float32 [4096, 64], P('seq', 'head'), may hold values from -2.4 to 2.4
- index_keys: bfloat16 [8192, 128], P('seq'), may hold values from -6 to 6
- index_outside: float32 [4096], P('seq'), may hold values from 6 to 10
- query_pos: int32 [4096], P('seq'), may hold values from 1 to 16383, as said below
- key_pos: int32 [8192], P('seq'), may hold values from 0 to 16383, as said below
Outputs:
- grad_index_query: bfloat16 [4096, 8192], P('seq', 'head')
- grad_index_weights: float32 [4096, 64], P('seq', 'head')
- grad_index_keys: float32 [8192, 128], P('seq')
The draws below stay inside these ranges and needn't reach their ends.
Inputs may be any that keep to these rules, and one draw needn't show every extreme that they name: `key_pos`: key j of block b stands at 2 * 256 * b + 2 * j or one more; key 0 of a block at 2 * 256 * b exactly. `query_pos`: queries of block b stand at 2 * 256 * b + 1 to 2 * 256 * b + 2 * 256 - 1.
All inputs are finite; a program needn't handle non-finite values.
Results may differ from the reference program's by a relative error of at most 0.00205.
Values may be sent and summed in bfloat16 or wider, within the bound.
A program may use at most 32 MiB of HBM per device.

```python
import jax
import jax.numpy as jnp
from jax import lax

HEADS = 128
LAT = 512
ROPE = 64
IHEADS = 64
IDIM = 128
Q_DEV = 128
KB = 256
STEPS = 4
QUERIES = 4096
KEYS = 8192
N_SEQ = 32


def draw_main_query(key, part):
    width = LAT + ROPE
    own_key = jax.random.fold_in(key, 31)
    base = jnp.clip(jax.random.normal(own_key, (QUERIES, HEADS, width), jnp.float32), -6.0, 6.0)
    return base.reshape(QUERIES, HEADS * width).astype(jnp.bfloat16)


def draw_latent(key, part):
    width = LAT + ROPE
    own_key = jax.random.fold_in(key, 37)
    base = jnp.clip(jax.random.normal(own_key, (KEYS, width), jnp.float32), -6.0, 6.0)
    return base.astype(jnp.bfloat16)


def draw_index_query(key, part):
    own_key = jax.random.fold_in(key, 41)
    base = jnp.clip(jax.random.normal(own_key, (QUERIES, IHEADS, IDIM), jnp.float32), -6.0, 6.0)
    return base.reshape(QUERIES, IHEADS * IDIM).astype(jnp.bfloat16)


def draw_index_weights(key, part):
    own_key = jax.random.fold_in(key, 43)
    base = jnp.clip(0.4 * jax.random.normal(own_key, (QUERIES, IHEADS), jnp.float32), -2.4, 2.4)
    return base.astype(jnp.float32)


def draw_index_keys(key, part):
    own_key = jax.random.fold_in(key, 47)
    base = jnp.clip(jax.random.normal(own_key, (KEYS, IDIM), jnp.float32), -6.0, 6.0)
    return base.astype(jnp.bfloat16)


def draw_key_pos(key, part):
    places = jnp.arange(KEYS, dtype=jnp.int32)
    inner = places % KB
    coins = jax.random.randint(jax.random.fold_in(key, 11), (KEYS,), 0, 2, dtype=jnp.int32)
    coins = jnp.where(inner == 0, 0, jnp.where(inner == KB - 1, 1, coins))
    return (places // KB * 2 * KB + 2 * inner + coins).astype(jnp.int32)


def draw_query_pos(key, part):
    places = jnp.arange(QUERIES, dtype=jnp.int32)
    inner = places % Q_DEV
    offsets = jax.random.randint(jax.random.fold_in(key, 13), (QUERIES,), 1, 2 * KB, dtype=jnp.int32)
    offsets = jnp.where(inner == 0, 1, jnp.where(inner == Q_DEV - 1, 2 * KB - 1, offsets))
    return (places // Q_DEV * 2 * KB + offsets).astype(jnp.int32)


def steps_of(rng, shape, shards, least, largest):
    level = 1.0
    for axis_at, parts in shards:
        draws = jax.random.uniform(jax.random.fold_in(jax.random.fold_in(rng, 6), axis_at), (parts,), jnp.float32, least / len(shards), largest / len(shards))
        level = level * jnp.repeat(jnp.exp(draws), shape[axis_at] // parts).reshape((-1,) + (1,) * (len(shape) - 1 - axis_at))
    return level


def setup_inputs(seed: int = 0) -> dict:
    key_of = jax.random.split(jax.random.key(seed), 10)
    return {
        "main_query": draw_main_query(jax.random.fold_in(key_of[9], 71), 0),
        "latent": draw_latent(jax.random.fold_in(key_of[9], 71), 0),
        "main_outside": jnp.clip(5.0 + 6.0 * jax.random.uniform(key_of[2], (QUERIES, HEADS), jnp.float32) ** steps_of(key_of[2], (QUERIES, HEADS), ((0, 32), (1, 32)), -0.2, 0.2), 5.0, 11.0),
        "index_query": draw_index_query(jax.random.fold_in(key_of[9], 71), 0),
        "index_weights": draw_index_weights(jax.random.fold_in(key_of[9], 71), 0),
        "index_keys": draw_index_keys(jax.random.fold_in(key_of[9], 71), 0),
        "index_outside": jnp.clip(6.0 + 4.0 * jax.random.uniform(key_of[6], (QUERIES,), jnp.float32) ** steps_of(key_of[6], (QUERIES,), ((0, 32),), -0.2, 0.2), 6.0, 10.0),
        "query_pos": draw_query_pos(jax.random.fold_in(key_of[9], 71), 0),
        "key_pos": draw_key_pos(jax.random.fold_in(key_of[9], 71), 0),
    }


NEGATIVE = -1e+30
SCORE_SCALE = 192.0 ** (-0.5)

def head_mass(scores, visible, outside):
    masked = jnp.where(visible[None], scores, NEGATIVE)
    highest = jnp.maximum(lax.optimization_barrier(jnp.max(masked, axis=2)), outside.T)
    expo = jnp.exp(masked - highest[:, :, None])
    total = lax.optimization_barrier(jnp.sum(expo, axis=2)) + jnp.exp(outside.T - highest)
    return lax.optimization_barrier(jnp.sum(expo / total[:, :, None], axis=0))

def score_grad(mass, index_score, visible, outside):
    target = mass / lax.optimization_barrier(jnp.sum(mass, axis=1, keepdims=True))
    masked = jnp.where(visible, index_score, NEGATIVE)
    highest = jnp.maximum(lax.optimization_barrier(jnp.max(masked, axis=1)), outside)
    expo = jnp.exp(masked - highest[:, None])
    total = lax.optimization_barrier(jnp.sum(expo, axis=1)) + jnp.exp(outside - highest)
    return (expo / total[:, None] - target) * (STEPS * KB)

def reference(main_query, latent, main_outside, index_query, index_weights, index_keys, index_outside, query_pos, key_pos):
    window = STEPS * KB
    front = (STEPS - 1) * KB
    latent_padded = jnp.concatenate([jnp.zeros((front, LAT + ROPE), latent.dtype), latent], 0)
    keys_padded = jnp.concatenate([jnp.zeros((front, IDIM), index_keys.dtype), index_keys], 0)
    places_padded = jnp.concatenate([jnp.zeros((front,), jnp.int32), key_pos.astype(jnp.int32)], 0)
    factor = IDIM ** (-0.5)
    slot_block = (jnp.arange(window, dtype=jnp.int32) // KB).astype(jnp.int32)
    lagging = (STEPS - 1 - slot_block).astype(jnp.int32)

    def one_block(grad_keys, block_index):
        first = (block_index * Q_DEV).astype(jnp.int32)
        key_first = (block_index * KB).astype(jnp.int32)
        queries = lax.dynamic_slice_in_dim(main_query, first, Q_DEV, 0).reshape(Q_DEV, HEADS, LAT + ROPE).astype(jnp.float32)
        latent_window = lax.dynamic_slice_in_dim(latent_padded, key_first, window, 0).astype(jnp.float32)
        key_window = lax.dynamic_slice_in_dim(keys_padded, key_first, window, 0)
        place_window = lax.dynamic_slice_in_dim(places_padded, key_first, window, 0)
        outside = lax.dynamic_slice_in_dim(main_outside, first, Q_DEV, 0)
        index_out = lax.dynamic_slice_in_dim(index_outside, first, Q_DEV, 0)
        query_places = lax.dynamic_slice_in_dim(query_pos.astype(jnp.int32), first, Q_DEV, 0)
        index_rows = lax.dynamic_slice_in_dim(index_query, first, Q_DEV, 0).reshape(Q_DEV, IHEADS, IDIM).astype(jnp.float32)
        weight_rows = lax.dynamic_slice_in_dim(index_weights, first, Q_DEV, 0)
        causal = (slot_block < STEPS - 1)[None, :] | (place_window[None, :] <= query_places[:, None])
        visible = (block_index >= lagging)[None, :] & causal
        scores = jnp.einsum('qhc,wc->hqw', queries, latent_window) * SCORE_SCALE
        mass = head_mass(scores, visible, outside)
        key_wide = key_window.astype(jnp.float32)
        activity = jnp.einsum('qjd,wd->jqw', index_rows, key_wide) * factor
        rectified = jnp.maximum(activity, 0.0)
        index_score = jnp.einsum('qj,jqw->qw', weight_rows, rectified)
        dscore = score_grad(mass, index_score, visible, index_out)
        gated = dscore[None] * weight_rows.T[:, :, None] * (activity > 0).astype(jnp.float32)
        grad_query = (jnp.einsum('jqw,wd->qjd', gated, key_wide, precision=lax.Precision.HIGHEST) * factor).astype(jnp.bfloat16)
        grad_weight = jnp.einsum('qw,jqw->qj', dscore, rectified)
        grad_key = jnp.einsum('jqw,qjd->wd', gated, index_rows, precision=lax.Precision.HIGHEST) * factor
        current = lax.dynamic_slice_in_dim(grad_keys, key_first, window, 0)
        grad_keys = lax.dynamic_update_slice_in_dim(grad_keys, current + grad_key, key_first, 0)
        return (grad_keys, (grad_query.reshape(Q_DEV, IHEADS * IDIM), grad_weight))
    start_keys = jnp.zeros((front + KEYS, IDIM), jnp.float32)
    grad_keys, stacked = lax.scan(one_block, start_keys, jnp.arange(N_SEQ, dtype=jnp.int32))
    grad_query = stacked[0].reshape(QUERIES, IHEADS * IDIM)
    grad_weight = stacked[1].reshape(QUERIES, IHEADS)
    return (grad_query, grad_weight, grad_keys[front:])
```

```python
import functools

import jax
import jax.numpy as jnp
from jax import lax
from jax.experimental import pallas as pl
from jax.experimental.pallas import tpu as pltpu
from jax.sharding import PartitionSpec as P

MESH = pl.DeviceIdType.MESH
STEPS = 4
IDIM = 128
WIDTH = 576
PAD = 64
WIDE = WIDTH + PAD
NEGATIVE = -1e30
ABSENT = 1e9
SCORE_SCALE = 192.0 ** (-0.5)
FACTOR = IDIM ** (-0.5)
F32 = jnp.float32
BF16 = jnp.bfloat16


def dot(a, b, dims):
    return lax.dot_general(a, b, (dims, ((), ())), preferred_element_type=F32)


def swap(x):
    return pltpu.roll(x, 4, 0)


def split_pair(a, b, low):
    return jnp.where(low, a, swap(b)), jnp.where(low, swap(a), b)


def high_part(x):
    return x.astype(BF16).astype(F32)


def kernel(
    ns,
    nh,
    main_query,
    latent,
    outside,
    index_query,
    index_weights,
    index_keys,
    index_outside,
    query_pos,
    key_pos,
    grad_query,
    grad_weight,
    grad_keys,
    rows,
    cols,
    place,
    queries,
    lat,
    keys,
    wide_query,
    scores,
    ask_out,
    ask_in,
    mass_out,
    mass_in,
    near_query,
    near_weight,
    act,
    upper,
    lower,
    rest_weight,
    terms_out,
    terms_in,
    back_out,
    back_in,
    part_out,
    part_in,
    final,
    wide_grad,
    weight_grad,
    local_sem,
    lat_send,
    lat_recv,
    key_send,
    key_recv,
    ask_sem,
    mass_sem,
    terms_sem,
    back_sem,
    part_send,
    part_recv,
    final_sem,
):
    q_rows = index_query.shape[0]
    kb = key_pos.shape[1]
    window = STEPS * kb
    half = window // 2
    chunks = q_rows // 8
    blocks = kb // 128
    tiles = 16 * blocks
    per = tiles // nh
    head = lax.axis_index("head")
    seq = lax.axis_index("seq")

    local = []
    for parity in range(2):
        for i in range(2):
            start = (2 * i + parity) * WIDTH - parity * PAD
            local.append(
                pltpu.make_async_copy(
                    main_query.at[:, pl.ds(start, WIDE)],
                    queries.at[parity, pl.ds(i * q_rows, q_rows), :],
                    local_sem.at[2 * parity + i],
                )
            )
    local.append(
        pltpu.make_async_copy(latent, lat.at[STEPS - 1, pl.ds(PAD, WIDTH), :], local_sem.at[4])
    )
    local.append(pltpu.make_async_copy(index_keys, keys.at[STEPS - 1], local_sem.at[5]))
    for copy in local:
        copy.start()

    barrier = pltpu.get_barrier_semaphore()

    def greet(r, carry):
        pl.semaphore_signal(
            barrier, inc=1, device_id={"head": lax.rem(head + r, nh)}, device_id_type=MESH
        )
        return carry

    for distance in range(1, STEPS):
        for other in (seq + distance, seq + ns - distance):
            pl.semaphore_signal(
                barrier, inc=1, device_id={"seq": lax.rem(other, ns)}, device_id_type=MESH
            )
    lax.fori_loop(1, nh, greet, 0)

    low = lax.broadcasted_iota(jnp.int32, (8, 128), 0) < 4
    lane = lax.broadcasted_iota(jnp.int32, (8, 128), 1)
    rows[...] = jnp.zeros_like(rows)
    rows[0:4, :] = outside[...]
    rows[4:6, :] = index_weights[...]
    rows[6:7, :] = query_pos[...].astype(F32)
    rows[7:8, :] = index_outside[...]
    cols[...] = rows[...].T
    for k in range(STEPS):
        here = jnp.where(seq >= STEPS - 1 - k, 0.0, ABSENT)
        own = key_pos[...].astype(F32) if k == STEPS - 1 else jnp.zeros((1, kb), F32)
        place[:, k * kb : (k + 1) * kb] = own + here
        lat[k, 0:PAD, :] = jnp.zeros((PAD, kb), BF16)
        lat[k, PAD + WIDTH : PAD + WIDTH + PAD, :] = jnp.zeros((PAD, kb), BF16)
    wide_query[...] = index_query[...].astype(F32)

    def ask(c, carry):
        at = pl.ds(pl.multiple_of(8 * c, 8), 8)
        values = wide_query[at, :]
        column = cols[at, :]
        first = jnp.broadcast_to(column[:, 4:5], (8, 128))
        second = jnp.broadcast_to(column[:, 5:6], (8, 128))
        pair = split_pair(values[:, :IDIM], values[:, IDIM:], low)
        weights = split_pair(first, second, low)
        for i in range(2):
            weight = weights[i]
            top = high_part(weight)
            mid = high_part(weight - top)
            end = weight - top - mid
            packed = jnp.where(lane == 0, top, jnp.where(lane == 1, mid, end))
            ask_out[2 * c + i] = jnp.concatenate([pair[i], packed], 0).astype(BF16)
        return carry

    lax.fori_loop(0, chunks, ask, 0)

    pl.semaphore_wait(barrier, nh - 1 + 2 * (STEPS - 1))

    lat_copies = []
    key_copies = []
    for distance in range(1, STEPS):
        target = {"seq": lax.rem(seq + distance, ns)}
        slot = STEPS - 1 - distance
        copy = pltpu.make_async_remote_copy(
            src_ref=latent,
            dst_ref=lat.at[slot, pl.ds(PAD, WIDTH), :],
            send_sem=lat_send.at[slot],
            recv_sem=lat_recv.at[slot],
            device_id=target,
            device_id_type=MESH,
        )
        copy.start()
        lat_copies.append(copy)
    for distance in range(1, STEPS):
        target = {"seq": lax.rem(seq + distance, ns)}
        slot = STEPS - 1 - distance
        copy = pltpu.make_async_remote_copy(
            src_ref=index_keys,
            dst_ref=keys.at[slot],
            send_sem=key_send.at[slot],
            recv_sem=key_recv.at[slot],
            device_id=target,
            device_id_type=MESH,
        )
        copy.start()
        key_copies.append(copy)

    def exchange(source, target, sems, peer, slot):
        return pltpu.make_async_remote_copy(
            src_ref=source,
            dst_ref=target,
            send_sem=sems.at[0],
            recv_sem=sems.at[1],
            device_id={"head": peer},
            device_id_type=MESH,
        )

    def send_ask(r, carry):
        peer = lax.rem(head + r, nh)
        exchange(ask_out.at[peer], ask_in.at[nh - 1 - r], ask_sem, peer, 0).start()
        return carry

    lax.fori_loop(1, nh, send_ask, 0)
    ask_in[nh - 1] = ask_out[head]

    def all_of(source, target, sems):
        return exchange(
            source.at[pl.ds(0, nh - 1)], target.at[pl.ds(0, nh - 1)], sems, lax.rem(head + 1, nh), 0
        )

    for copy in local:
        copy.wait()
    for k in range(STEPS - 1, -1, -1):
        if k < STEPS - 1:
            lat_copies[STEPS - 2 - k].wait_recv()
        for parity in range(2):
            table = lat[k, PAD * (1 - parity) : PAD * (1 - parity) + WIDE, :]
            scores[parity, :, k * kb : (k + 1) * kb] = (
                dot(queries[parity], table, ((1,), (0,))) * SCORE_SCALE
            )

    def soften(step, carry):
        c = lax.rem(step + head // 2 + 1, chunks)
        at = pl.ds(pl.multiple_of(8 * c, 8), 8)
        column = cols[at, :]
        visible = place[...] <= column[:, 6:7]
        mass = jnp.zeros((8, window), F32)
        for parity in range(2):
            for i in range(2):
                h = 2 * i + parity
                from_row = pl.multiple_of(i * q_rows + 8 * c, 8)
                x = jnp.where(visible, scores[parity, pl.ds(from_row, 8), :], NEGATIVE)
                out = column[:, h : h + 1]
                top = jnp.maximum(jnp.max(x, axis=1, keepdims=True), out)
                e = jnp.exp(x - top)
                total = jnp.sum(e, axis=1, keepdims=True) + jnp.exp(out - top)
                mass = mass + e * (1.0 / total)
        halves = split_pair(
            mass[:, :half], mass[:, half:], lax.broadcasted_iota(jnp.int32, (8, half), 0) < 4
        )
        for i in range(2):
            peer = 2 * c + i
            mass_out[peer] = halves[i]

            @pl.when(peer != head)
            def _():
                r = lax.rem(peer + nh - head, nh)
                exchange(mass_out.at[peer], mass_in.at[nh - 1 - r], mass_sem, peer, 0).start()

        return carry

    lax.fori_loop(0, chunks, soften, 0)
    mass_in[nh - 1] = mass_out[head]

    all_of(ask_out, ask_in, ask_sem).wait_recv()

    def unpack(g, carry):
        at = pl.ds(pl.multiple_of(8 * g, 8), 8)
        both = ask_in[g].astype(F32)
        near_query[at, :] = both[0:8, :]
        packed = both[8:16, :]
        weight = packed[:, 0:1] + (packed[:, 1:2] + packed[:, 2:3])
        near_weight[at, :] = jnp.broadcast_to(weight, (8, 128))
        return carry

    lax.fori_loop(0, nh, unpack, 0)
    asked = near_query[...].astype(BF16)
    for k in range(STEPS - 1, -1, -1):
        if k < STEPS - 1:
            key_copies[STEPS - 2 - k].wait_recv()
        act[:, k * kb : (k + 1) * kb] = dot(asked, keys[k], ((1,), (1,))) * FACTOR

    def add_score(g, total):
        at = pl.ds(pl.multiple_of(8 * g, 8), 8)
        return total + near_weight[at, 0:1] * jnp.maximum(act[at, :], 0.0)

    score = lax.fori_loop(0, nh, add_score, jnp.zeros((8, window), F32))
    score = score + swap(score)
    odd = lax.rem(head, 2)
    column = cols[pl.ds(pl.multiple_of(8 * (head // 2), 8), 8), :]
    pick = (lax.broadcasted_iota(jnp.int32, (8, 128), 0) // 4) == odd
    column = jnp.where(pick, column, swap(column))
    visible = place[...] <= column[:, 6:7]
    masked = jnp.where(visible, score, NEGATIVE)
    limit = column[:, 7:8]
    top = jnp.maximum(jnp.max(masked, axis=1, keepdims=True), limit)
    e = jnp.exp(masked - top)
    total = jnp.sum(e, axis=1, keepdims=True) + jnp.exp(limit - top)
    predicted = e * (1.0 / total)
    weighted = near_weight[...] * near_query[...]
    turned = weighted.T
    turned_high = turned.astype(BF16)
    turned_low = (turned - turned_high.astype(F32)).astype(BF16)

    all_of(mass_out, mass_in, mass_sem).wait_recv()
    mass = mass_in[0]
    for g in range(1, nh):
        mass = mass + mass_in[g]
    low_half = lax.broadcasted_iota(jnp.int32, (8, half), 0) < 4
    turned_mass = swap(mass)
    mass = jnp.concatenate(
        [jnp.where(low_half, mass, turned_mass), jnp.where(low_half, turned_mass, mass)], 1
    )
    target = mass * (1.0 / jnp.sum(mass, axis=1, keepdims=True))
    dscore = (predicted - target) * float(window)
    d_high = high_part(dscore)
    d_low = dscore - d_high

    def gate(g, carry):
        at = pl.ds(pl.multiple_of(16 * g, 16), 16)
        a = act[at, :]
        on = a > 0.0
        upper[at, :] = jnp.where(on, jnp.concatenate([d_high, d_high], 0), 0.0).astype(BF16)
        lower[at, :] = jnp.where(on, jnp.concatenate([d_low, d_low], 0), 0.0).astype(BF16)
        share = jnp.sum(
            jnp.concatenate([dscore, dscore], 0) * jnp.maximum(a, 0.0), axis=1, keepdims=True
        )
        rest_weight[at, :] = jnp.broadcast_to(share, (16, 128))
        return carry

    lax.fori_loop(0, nh // 2, gate, 0)

    for k in range(STEPS):
        at = slice(k * kb, (k + 1) * kb)
        high_block = upper[:, at]
        terms = dot(turned_high, high_block, ((1,), (0,)))
        terms = terms + dot(turned_low, high_block, ((1,), (0,)))
        terms = terms + dot(turned_high, lower[:, at], ((1,), (0,)))
        terms = terms * FACTOR
        for tile in range(tiles):
            d, b = tile // blocks, tile % blocks
            terms_out[tile // per, k, tile % per] = terms[
                8 * d : 8 * d + 8, 128 * b : 128 * b + 128
            ]

    def send_terms(r, carry):
        peer = lax.rem(head + r, nh)
        exchange(terms_out.at[peer], terms_in.at[nh - 1 - r], terms_sem, peer, 0).start()
        return carry

    lax.fori_loop(1, nh, send_terms, 0)
    terms_in[nh - 1] = terms_out[head]

    all_keys = keys[...].reshape(window, IDIM)
    near_grad = dot(upper[...], all_keys, ((1,), (0,))) + dot(lower[...], all_keys, ((1,), (0,)))
    wide_grad[...] = near_grad * FACTOR * near_weight[...]

    def pack_back(g, carry):
        at = pl.ds(pl.multiple_of(8 * g, 8), 8)
        share = rest_weight[at, :]
        top = high_part(share)
        mid = high_part(share - top)
        packed = jnp.where(lane == 0, top, jnp.where(lane == 1, mid, share - top - mid))
        back_out[g] = jnp.concatenate([wide_grad[at, :], packed], 0).astype(BF16)
        return carry

    lax.fori_loop(0, nh, pack_back, 0)

    def send_back(r, carry):
        peer = lax.rem(head + r, nh)
        exchange(back_out.at[r - 1], back_in.at[head], back_sem, peer, 0).start()
        return carry

    lax.fori_loop(1, nh, send_back, 0)
    back_in[head] = back_out[nh - 1]

    all_of(terms_out, terms_in, terms_sem).wait_recv()
    summed = terms_in[0]
    for g in range(1, nh):
        summed = summed + terms_in[g]
    part_out[...] = summed
    part_copies = []
    for k in range(STEPS - 1):
        distance = STEPS - 1 - k
        copy = pltpu.make_async_remote_copy(
            src_ref=part_out.at[k],
            dst_ref=part_in.at[k],
            send_sem=part_send.at[k],
            recv_sem=part_recv.at[k],
            device_id={"seq": lax.rem(seq + ns - distance, ns)},
            device_id_type=MESH,
        )
        copy.start()
        part_copies.append(copy)
    mine = part_out[STEPS - 1]
    for copy in part_copies:
        copy.wait_recv()
    for k in range(STEPS - 1):
        mine = mine + part_in[k]
    final[head] = mine

    def send_final(r, carry):
        peer = lax.rem(head + r, nh)
        exchange(final.at[head], final.at[head], final_sem, peer, 0).start()
        return carry

    lax.fori_loop(1, nh, send_final, 0)

    all_of(back_out, back_in, back_sem).wait_recv()

    def unpack_back(c, carry):
        at = pl.ds(pl.multiple_of(8 * c, 8), 8)
        one = back_in[2 * c].astype(F32)
        two = back_in[2 * c + 1].astype(F32)
        first, second = split_pair(one[0:8, :], two[0:8, :], low)
        wide_query[at, 0:IDIM] = first
        wide_query[at, IDIM : 2 * IDIM] = second
        shares = []
        for packed in (one[8:16, :], two[8:16, :]):
            share = packed[:, 0:1] + (packed[:, 1:2] + packed[:, 2:3])
            shares.append(jnp.broadcast_to(share, (8, 128)))
        first, second = split_pair(shares[0], shares[1], low)
        weight_grad[at, :] = jnp.where(lane == 0, first, second)
        return carry

    lax.fori_loop(0, chunks, unpack_back, 0)
    grad_query[...] = wide_query[...].astype(BF16)
    grad_weight[...] = weight_grad[...].T[0:2, :]

    all_of(final, final, final_sem).wait_recv()
    for b in range(blocks):
        columns = [final[(d * blocks + b) // per, (d * blocks + b) % per] for d in range(16)]
        grad_keys[128 * b : 128 * b + 128, :] = jnp.concatenate(columns, 0).T

    for copy in lat_copies + key_copies + part_copies:
        copy.wait_send()
    all_of(ask_out, ask_in, ask_sem).wait_send()
    all_of(mass_out, mass_in, mass_sem).wait_send()
    all_of(terms_out, terms_in, terms_sem).wait_send()
    all_of(back_out, back_in, back_sem).wait_send()
    all_of(final, final, final_sem).wait_send()


def solution(mesh):
    ns, nh = mesh.shape["seq"], mesh.shape["head"]

    def shards(
        main_query,
        latent,
        main_outside,
        index_query,
        index_weights,
        index_keys,
        index_outside,
        query_pos,
        key_pos,
    ):
        q = main_query.shape[0]
        kb = latent.shape[0]
        window = STEPS * kb
        per = 16 * (kb // 128) // nh
        vmem = pl.BlockSpec(memory_space=pltpu.VMEM)
        whole = pl.BlockSpec(memory_space=pl.ANY)
        dma = pltpu.SemaphoreType.DMA
        grad_query, grad_weight, grad_keys = pl.pallas_call(
            functools.partial(kernel, ns, nh),
            out_shape=(
                jax.ShapeDtypeStruct((q, 2 * IDIM), BF16),
                jax.ShapeDtypeStruct((2, q), F32),
                jax.ShapeDtypeStruct((kb, IDIM), F32),
            ),
            in_specs=[whole, whole, vmem, vmem, vmem, whole, vmem, vmem, vmem],
            out_specs=(vmem, vmem, vmem),
            scratch_shapes=[
                pltpu.VMEM((128, q), F32),
                pltpu.VMEM((q, 128), F32),
                pltpu.VMEM((1, window), F32),
                pltpu.VMEM((2, 2 * q, WIDE), BF16),
                pltpu.VMEM((STEPS, WIDE + PAD, kb), BF16),
                pltpu.VMEM((STEPS, kb, IDIM), BF16),
                pltpu.VMEM((q, 2 * IDIM), F32),
                pltpu.VMEM((2, 2 * q, window), F32),
                pltpu.VMEM((nh, 16, 128), BF16),
                pltpu.VMEM((nh, 16, 128), BF16),
                pltpu.VMEM((nh, 8, window // 2), F32),
                pltpu.VMEM((nh, 8, window // 2), F32),
                pltpu.VMEM((8 * nh, 128), F32),
                pltpu.VMEM((8 * nh, 128), F32),
                pltpu.VMEM((8 * nh, window), F32),
                pltpu.VMEM((8 * nh, window), BF16),
                pltpu.VMEM((8 * nh, window), BF16),
                pltpu.VMEM((8 * nh, 128), F32),
                pltpu.VMEM((nh, STEPS, per, 8, 128), F32),
                pltpu.VMEM((nh, STEPS, per, 8, 128), F32),
                pltpu.VMEM((nh, 16, 128), BF16),
                pltpu.VMEM((nh, 16, 128), BF16),
                pltpu.VMEM((STEPS, per, 8, 128), F32),
                pltpu.VMEM((STEPS - 1, per, 8, 128), F32),
                pltpu.VMEM((nh, per, 8, 128), F32),
                pltpu.VMEM((8 * nh, 128), F32),
                pltpu.VMEM((q, 128), F32),
                dma((6,)),
                dma((STEPS - 1,)),
                dma((STEPS - 1,)),
                dma((STEPS - 1,)),
                dma((STEPS - 1,)),
                dma((2,)),
                dma((2,)),
                dma((2,)),
                dma((2,)),
                dma((STEPS - 1,)),
                dma((STEPS - 1,)),
                dma((2,)),
            ],
            compiler_params=pltpu.CompilerParams(
                collective_id=0, has_side_effects=True, vmem_limit_bytes=48 << 20
            ),
        )(
            main_query,
            latent.T,
            main_outside.T,
            index_query,
            index_weights.T,
            index_keys,
            index_outside.reshape(1, q),
            query_pos.reshape(1, q),
            key_pos.reshape(1, kb),
        )
        return grad_query, grad_weight.T, grad_keys

    in_specs = (
        P("seq", "head"),
        P("seq", None),
        P("seq", "head"),
        P("seq", "head"),
        P("seq", "head"),
        P("seq", None),
        P("seq"),
        P("seq"),
        P("seq"),
    )
    out_specs = (P("seq", "head"), P("seq", "head"), P("seq", None))
    return jax.shard_map(shards, mesh=mesh, in_specs=in_specs, out_specs=out_specs, check_vma=False)
```

```python
import functools

import jax
import jax.numpy as jnp
from jax import lax
from jax.experimental import pallas as pl
from jax.experimental.pallas import tpu as pltpu
from jax.sharding import PartitionSpec as P

MESH = pl.DeviceIdType.MESH
STEPS = 4
IDIM = 128
WIDTH = 576
PAD = 64
WIDE = WIDTH + PAD
X_RUN = 4
X_ROWS = 320
Z_ROWS = WIDTH - X_ROWS
NEGATIVE = -1e30
ABSENT = 1e9
SCORE_SCALE = 192.0 ** (-0.5)
FACTOR = IDIM ** (-0.5)
F32 = jnp.float32
BF16 = jnp.bfloat16


def dot(a, b, dims):
    return lax.dot_general(a, b, (dims, ((), ())), preferred_element_type=F32)


def swap(x):
    return pltpu.roll(x, 4, 0)


def split_pair(a, b, low):
    return jnp.where(low, a, swap(b)), jnp.where(low, swap(a), b)


def high_part(x):
    return x.astype(BF16).astype(F32)


def kernel(
    ns,
    nh,
    main_query,
    latent,
    outside,
    index_query,
    index_weights,
    index_keys,
    index_outside,
    query_pos,
    key_pos,
    grad_query,
    grad_weight,
    grad_keys,
    rows,
    cols,
    place,
    queries,
    lat,
    keys,
    narrow_query,
    wide_query,
    scores,
    ask_out,
    ask_in,
    mass_out,
    mass_in,
    near_query,
    near_weight,
    act,
    upper,
    lower,
    rest_weight,
    terms_out,
    terms_in,
    back_out,
    back_in,
    part_out,
    part_in,
    final,
    wide_grad,
    weight_grad,
    local_sem,
    cross_send,
    cross_recv,
    direct_send,
    direct_recv,
    gather_send,
    gather_recv,
    forward_send,
    forward_recv,
    ask_sem,
    mass_sem,
    terms_sem,
    back_sem,
    part_send,
    part_recv,
    final_sem,
):
    q_rows = index_query.shape[0]
    kb = key_pos.shape[1]
    window = STEPS * kb
    half = window // 2
    chunks = q_rows // 8
    blocks = kb // 128
    tiles = 16 * blocks
    per = tiles // nh
    head = lax.axis_index("head")
    seq = lax.axis_index("seq")

    local = []
    for parity in range(2):
        for i in range(2):
            start = (2 * i + parity) * WIDTH - parity * PAD
            local.append(
                pltpu.make_async_copy(
                    main_query.at[:, pl.ds(start, WIDE)],
                    queries.at[parity, pl.ds(i * q_rows, q_rows), :],
                    local_sem.at[2 * parity + i],
                )
            )
    local.append(
        pltpu.make_async_copy(latent, lat.at[STEPS - 1, pl.ds(PAD, WIDTH), :], local_sem.at[4])
    )
    local.append(pltpu.make_async_copy(index_keys, keys.at[STEPS - 1], local_sem.at[5]))
    local.append(pltpu.make_async_copy(index_query, narrow_query, local_sem.at[6]))
    for copy in local:
        copy.start()

    barrier = pltpu.get_barrier_semaphore()

    def greet(r, carry):
        pl.semaphore_signal(
            barrier, inc=1, device_id={"head": lax.rem(head + r, nh)}, device_id_type=MESH
        )
        return carry

    for distance in range(1, STEPS):
        for other in (seq + distance, seq + ns - distance):
            pl.semaphore_signal(
                barrier, inc=1, device_id={"seq": lax.rem(other, ns)}, device_id_type=MESH
            )
    lax.fori_loop(1, nh, greet, 0)

    low = lax.broadcasted_iota(jnp.int32, (8, 128), 0) < 4
    lane = lax.broadcasted_iota(jnp.int32, (8, 128), 1)
    rows[...] = jnp.zeros_like(rows)
    rows[0:4, :] = outside[...]
    rows[4:6, :] = index_weights[...]
    rows[6:7, :] = query_pos[...].astype(F32)
    rows[7:8, :] = index_outside[...]
    cols[...] = rows[...].T
    for k in range(STEPS):
        here = jnp.where(seq >= STEPS - 1 - k, 0.0, ABSENT)
        own = key_pos[...].astype(F32) if k == STEPS - 1 else jnp.zeros((1, kb), F32)
        place[:, k * kb : (k + 1) * kb] = own + here
        lat[k, 0:PAD, :] = jnp.zeros((PAD, kb), BF16)
        lat[k, PAD + WIDTH : PAD + WIDTH + PAD, :] = jnp.zeros((PAD, kb), BF16)
    local[6].wait()
    wide_query[...] = narrow_query[...].astype(F32)

    def ask(c, carry):
        at = pl.ds(pl.multiple_of(8 * c, 8), 8)
        values = wide_query[at, :]
        column = cols[at, :]
        first = jnp.broadcast_to(column[:, 4:5], (8, 128))
        second = jnp.broadcast_to(column[:, 5:6], (8, 128))
        pair = split_pair(values[:, :IDIM], values[:, IDIM:], low)
        weights = split_pair(first, second, low)
        for i in range(2):
            weight = weights[i]
            top = high_part(weight)
            mid = high_part(weight - top)
            end = weight - top - mid
            packed = jnp.where(lane == 0, top, jnp.where(lane == 1, mid, end))
            ask_out[2 * c + i] = jnp.concatenate([pair[i], packed], 0).astype(BF16)
        return carry

    lax.fori_loop(0, chunks, ask, 0)

    pl.semaphore_wait(barrier, nh - 1 + 2 * (STEPS - 1))

    core = lax.rem(seq, 2)
    early, late = 2 * core, 2 - 2 * core
    ring, run = head // X_RUN, lax.rem(head, X_RUN)
    rings = nh // X_RUN
    run_rows, ring_rows, key_rows = X_ROWS // X_RUN, Z_ROWS // rings, kb // rings
    run_at = pl.multiple_of(run_rows * run, 16)
    ring_at = pl.multiple_of(X_ROWS + ring_rows * ring, 16)
    key_at = pl.multiple_of(key_rows * ring, 16)

    def lat_rows(slot, start, size):
        return lat.at[slot, pl.ds(pl.multiple_of(PAD + start, 16), size), :]

    def key_part(slot, start, size):
        return keys.at[slot, pl.ds(start, size), :]

    def to_seq(source, target, send, recv, i, other):
        return pltpu.make_async_remote_copy(
            src_ref=source,
            dst_ref=target,
            send_sem=send.at[i],
            recv_sem=recv.at[i],
            device_id={"seq": other},
            device_id_type=MESH,
        )

    two = lax.rem(seq + 2, ns)
    sibling = seq + 1 - 2 * core
    crossing = [
        to_seq(
            index_keys.at[pl.ds(key_at, key_rows), :],
            key_part(1, key_at, key_rows),
            cross_send, cross_recv, 0, two,
        ),
        to_seq(
            latent.at[pl.ds(ring_at, ring_rows), :],
            lat_rows(1, ring_at, ring_rows),
            cross_send, cross_recv, 1, two,
        ),
        to_seq(
            latent.at[pl.ds(run_at, run_rows), :],
            lat_rows(1, run_at, run_rows),
            cross_send, cross_recv, 2, two,
        ),
    ]
    onward = lax.rem(seq + 1 + 2 * core, ns)
    direct = [
        to_seq(index_keys, keys.at[late], direct_send, direct_recv, 0, onward),
        to_seq(latent, lat_rows(late, 0, WIDTH), direct_send, direct_recv, 1, onward),
    ]
    for copy in crossing + direct:
        copy.start()

    def exchange(source, target, sems, peer, slot):
        return pltpu.make_async_remote_copy(
            src_ref=source,
            dst_ref=target,
            send_sem=sems.at[0],
            recv_sem=sems.at[1],
            device_id={"head": peer},
            device_id_type=MESH,
        )

    def send_ask(r, carry):
        peer = lax.rem(head + r, nh)
        exchange(ask_out.at[peer], ask_in.at[nh - 1 - r], ask_sem, peer, 0).start()
        return carry

    lax.fori_loop(1, nh, send_ask, 0)
    ask_in[nh - 1] = ask_out[head]

    def all_of(source, target, sems):
        return exchange(
            source.at[pl.ds(0, nh - 1)], target.at[pl.ds(0, nh - 1)], sems, lax.rem(head + 1, nh), 0
        )

    def score_block(k):
        at = pl.ds(pl.multiple_of(k * kb, 128), kb)
        for parity in range(2):
            table = lat[k, PAD * (1 - parity) : PAD * (1 - parity) + WIDE, :]
            scores[parity, :, at] = dot(queries[parity], table, ((1,), (0,))) * SCORE_SCALE

    def act_block(k, asked):
        at = pl.ds(pl.multiple_of(k * kb, 128), kb)
        act[:, at] = dot(asked, keys[k], ((1,), (1,))) * FACTOR

    def to_head(part, i, peer):
        return pltpu.make_async_remote_copy(
            src_ref=part,
            dst_ref=part,
            send_sem=gather_send.at[i],
            recv_sem=gather_recv.at[i],
            device_id={"head": peer},
            device_id_type=MESH,
        )

    for copy in local[:6]:
        copy.wait()
    score_block(STEPS - 1)
    for copy in crossing:
        copy.wait_recv()

    def push_ring(r, carry):
        peer = lax.rem(head + r * X_RUN, nh)
        to_head(key_part(1, key_at, key_rows), 0, peer).start()
        to_head(lat_rows(1, ring_at, ring_rows), 1, peer).start()
        return carry

    def push_run(r, carry):
        peer = ring * X_RUN + lax.rem(run + r, X_RUN)
        to_head(lat_rows(1, run_at, run_rows), 2, peer).start()
        return carry

    lax.fori_loop(1, rings, push_ring, 0)
    lax.fori_loop(1, X_RUN, push_run, 0)
    gathered = [
        to_head(key_part(1, 0, key_rows * (rings - 1)), 0, head),
        to_head(lat_rows(1, 0, ring_rows * (rings - 1)), 1, head),
        to_head(lat_rows(1, 0, run_rows * (X_RUN - 1)), 2, head),
    ]
    forward = [
        to_seq(keys.at[1], keys.at[early], forward_send, forward_recv, 0, sibling),
        to_seq(
            lat_rows(1, X_ROWS, Z_ROWS),
            lat_rows(early, X_ROWS, Z_ROWS),
            forward_send, forward_recv, 1, sibling,
        ),
        to_seq(
            lat_rows(1, 0, X_ROWS),
            lat_rows(early, 0, X_ROWS),
            forward_send, forward_recv, 2, sibling,
        ),
    ]
    for copy in direct:
        copy.wait_recv()
    score_block(early)
    for i in range(3):
        gathered[i].wait_recv()
        forward[i].start()
    score_block(1)

    all_of(ask_out, ask_in, ask_sem).wait_recv()

    def unpack(g, carry):
        at = pl.ds(pl.multiple_of(8 * g, 8), 8)
        both = ask_in[g].astype(F32)
        near_query[at, :] = both[0:8, :]
        packed = both[8:16, :]
        weight = packed[:, 0:1] + (packed[:, 1:2] + packed[:, 2:3])
        near_weight[at, :] = jnp.broadcast_to(weight, (8, 128))
        return carry

    lax.fori_loop(0, nh, unpack, 0)
    asked = near_query[...].astype(BF16)
    act_block(STEPS - 1, asked)
    act_block(early, asked)
    act_block(1, asked)
    forward[1].wait_recv()
    forward[2].wait_recv()
    score_block(late)

    def soften(step, carry):
        c = lax.rem(step + head // 2 + 1, chunks)
        at = pl.ds(pl.multiple_of(8 * c, 8), 8)
        column = cols[at, :]
        visible = place[...] <= column[:, 6:7]
        mass = jnp.zeros((8, window), F32)
        for parity in range(2):
            for i in range(2):
                h = 2 * i + parity
                from_row = pl.multiple_of(i * q_rows + 8 * c, 8)
                x = jnp.where(visible, scores[parity, pl.ds(from_row, 8), :], NEGATIVE)
                out = column[:, h : h + 1]
                top = jnp.maximum(jnp.max(x, axis=1, keepdims=True), out)
                e = jnp.exp(x - top)
                total = jnp.sum(e, axis=1, keepdims=True) + jnp.exp(out - top)
                mass = mass + e * (1.0 / total)
        halves = split_pair(
            mass[:, :half], mass[:, half:], lax.broadcasted_iota(jnp.int32, (8, half), 0) < 4
        )
        for i in range(2):
            peer = 2 * c + i
            mass_out[peer] = jnp.concatenate(
                [halves[i][:, : half // 2], halves[i][:, half // 2 :]], 0
            ).astype(BF16)

            @pl.when(peer != head)
            def _():
                r = lax.rem(peer + nh - head, nh)
                exchange(mass_out.at[peer], mass_in.at[nh - 1 - r], mass_sem, peer, 0).start()

        return carry

    lax.fori_loop(0, chunks, soften, 0)
    mass_in[nh - 1] = mass_out[head]

    forward[0].wait_recv()
    act_block(late, asked)

    def add_score(g, total):
        at = pl.ds(pl.multiple_of(8 * g, 8), 8)
        return total + near_weight[at, 0:1] * jnp.maximum(act[at, :], 0.0)

    score = lax.fori_loop(0, nh, add_score, jnp.zeros((8, window), F32))
    score = score + swap(score)
    odd = lax.rem(head, 2)
    column = cols[pl.ds(pl.multiple_of(8 * (head // 2), 8), 8), :]
    pick = (lax.broadcasted_iota(jnp.int32, (8, 128), 0) // 4) == odd
    column = jnp.where(pick, column, swap(column))
    visible = place[...] <= column[:, 6:7]
    masked = jnp.where(visible, score, NEGATIVE)
    limit = column[:, 7:8]
    top = jnp.maximum(jnp.max(masked, axis=1, keepdims=True), limit)
    e = jnp.exp(masked - top)
    total = jnp.sum(e, axis=1, keepdims=True) + jnp.exp(limit - top)
    predicted = e * (1.0 / total)
    weighted = near_weight[...] * near_query[...]
    turned = weighted.T
    turned_high = turned.astype(BF16)
    turned_low = (turned - turned_high.astype(F32)).astype(BF16)

    all_of(mass_out, mass_in, mass_sem).wait_recv()
    mass = mass_in[0].astype(F32)
    for g in range(1, nh):
        mass = mass + mass_in[g].astype(F32)
    mass = jnp.concatenate([mass[0:8, :], mass[8:16, :]], 1)
    low_half = lax.broadcasted_iota(jnp.int32, (8, half), 0) < 4
    turned_mass = swap(mass)
    mass = jnp.concatenate(
        [jnp.where(low_half, mass, turned_mass), jnp.where(low_half, turned_mass, mass)], 1
    )
    target = mass * (1.0 / jnp.sum(mass, axis=1, keepdims=True))
    dscore = (predicted - target) * float(window)
    d_high = high_part(dscore)
    d_low = dscore - d_high

    def gate(g, carry):
        at = pl.ds(pl.multiple_of(16 * g, 16), 16)
        a = act[at, :]
        on = a > 0.0
        upper[at, :] = jnp.where(on, jnp.concatenate([d_high, d_high], 0), 0.0).astype(BF16)
        lower[at, :] = jnp.where(on, jnp.concatenate([d_low, d_low], 0), 0.0).astype(BF16)
        share = jnp.sum(
            jnp.concatenate([dscore, dscore], 0) * jnp.maximum(a, 0.0), axis=1, keepdims=True
        )
        rest_weight[at, :] = jnp.broadcast_to(share, (16, 128))
        return carry

    lax.fori_loop(0, nh // 2, gate, 0)

    for k in range(STEPS):
        at = slice(k * kb, (k + 1) * kb)
        high_block = upper[:, at]
        terms = dot(turned_high, high_block, ((1,), (0,)))
        terms = terms + dot(turned_low, high_block, ((1,), (0,)))
        terms = terms + dot(turned_high, lower[:, at], ((1,), (0,)))
        terms = terms * FACTOR
        for tile in range(tiles):
            d, b = tile // blocks, tile % blocks
            terms_out[tile // per, k, tile % per] = terms[
                8 * d : 8 * d + 8, 128 * b : 128 * b + 128
            ]

    def send_terms(r, carry):
        peer = lax.rem(head + r, nh)
        exchange(terms_out.at[peer], terms_in.at[nh - 1 - r], terms_sem, peer, 0).start()
        return carry

    lax.fori_loop(1, nh, send_terms, 0)
    terms_in[nh - 1] = terms_out[head]

    all_keys = keys[...].reshape(window, IDIM)
    near_grad = dot(upper[...], all_keys, ((1,), (0,))) + dot(lower[...], all_keys, ((1,), (0,)))
    wide_grad[...] = near_grad * FACTOR * near_weight[...]

    def pack_back(g, carry):
        at = pl.ds(pl.multiple_of(8 * g, 8), 8)
        share = rest_weight[at, :]
        top = high_part(share)
        mid = high_part(share - top)
        packed = jnp.where(lane == 0, top, jnp.where(lane == 1, mid, share - top - mid))
        back_out[g] = jnp.concatenate([wide_grad[at, :], packed], 0).astype(BF16)
        return carry

    lax.fori_loop(0, nh, pack_back, 0)

    def send_back(r, carry):
        peer = lax.rem(head + r, nh)
        exchange(back_out.at[r - 1], back_in.at[head], back_sem, peer, 0).start()
        return carry

    lax.fori_loop(1, nh, send_back, 0)
    back_in[head] = back_out[nh - 1]

    all_of(terms_out, terms_in, terms_sem).wait_recv()
    summed = terms_in[0]
    for g in range(1, nh):
        summed = summed + terms_in[g]
    part_out[...] = summed
    part_copies = []
    for k in range(STEPS - 1):
        distance = STEPS - 1 - k
        copy = pltpu.make_async_remote_copy(
            src_ref=part_out.at[k],
            dst_ref=part_in.at[k],
            send_sem=part_send.at[k],
            recv_sem=part_recv.at[k],
            device_id={"seq": lax.rem(seq + ns - distance, ns)},
            device_id_type=MESH,
        )
        copy.start()
        part_copies.append(copy)
    mine = part_out[STEPS - 1]
    for copy in part_copies:
        copy.wait_recv()
    for k in range(STEPS - 1):
        mine = mine + part_in[k]
    final[head] = mine

    def send_final(r, carry):
        peer = lax.rem(head + r, nh)
        exchange(final.at[head], final.at[head], final_sem, peer, 0).start()
        return carry

    lax.fori_loop(1, nh, send_final, 0)

    all_of(back_out, back_in, back_sem).wait_recv()

    def unpack_back(c, carry):
        at = pl.ds(pl.multiple_of(8 * c, 8), 8)
        one = back_in[2 * c].astype(F32)
        two = back_in[2 * c + 1].astype(F32)
        first, second = split_pair(one[0:8, :], two[0:8, :], low)
        wide_query[at, 0:IDIM] = first
        wide_query[at, IDIM : 2 * IDIM] = second
        shares = []
        for packed in (one[8:16, :], two[8:16, :]):
            share = packed[:, 0:1] + (packed[:, 1:2] + packed[:, 2:3])
            shares.append(jnp.broadcast_to(share, (8, 128)))
        first, second = split_pair(shares[0], shares[1], low)
        weight_grad[at, :] = jnp.where(lane == 0, first, second)
        return carry

    lax.fori_loop(0, chunks, unpack_back, 0)
    grad_query[...] = wide_query[...].astype(BF16)
    grad_weight[...] = weight_grad[...].T[0:2, :]

    all_of(final, final, final_sem).wait_recv()
    for b in range(blocks):
        columns = [final[(d * blocks + b) // per, (d * blocks + b) % per] for d in range(16)]
        grad_keys[128 * b : 128 * b + 128, :] = jnp.concatenate(columns, 0).T

    for copy in crossing + direct + gathered + forward + part_copies:
        copy.wait_send()
    all_of(ask_out, ask_in, ask_sem).wait_send()
    all_of(mass_out, mass_in, mass_sem).wait_send()
    all_of(terms_out, terms_in, terms_sem).wait_send()
    all_of(back_out, back_in, back_sem).wait_send()
    all_of(final, final, final_sem).wait_send()


def solution(mesh):
    ns, nh = mesh.shape["seq"], mesh.shape["head"]

    def shards(
        main_query,
        latent,
        main_outside,
        index_query,
        index_weights,
        index_keys,
        index_outside,
        query_pos,
        key_pos,
    ):
        q = main_query.shape[0]
        kb = latent.shape[0]
        window = STEPS * kb
        per = 16 * (kb // 128) // nh
        vmem = pl.BlockSpec(memory_space=pltpu.VMEM)
        whole = pl.BlockSpec(memory_space=pltpu.MemorySpace.HBM)
        dma = pltpu.SemaphoreType.DMA
        grad_query, grad_weight, grad_keys = pl.pallas_call(
            functools.partial(kernel, ns, nh),
            out_shape=(
                jax.ShapeDtypeStruct((q, 2 * IDIM), BF16),
                jax.ShapeDtypeStruct((2, q), F32),
                jax.ShapeDtypeStruct((kb, IDIM), F32),
            ),
            in_specs=[whole, whole, vmem, whole, vmem, whole, vmem, vmem, vmem],
            out_specs=(vmem, vmem, vmem),
            scratch_shapes=[
                pltpu.VMEM((128, q), F32),
                pltpu.VMEM((q, 128), F32),
                pltpu.VMEM((1, window), F32),
                pltpu.VMEM((2, 2 * q, WIDE), BF16),
                pltpu.VMEM((STEPS, WIDE + PAD, kb), BF16),
                pltpu.VMEM((STEPS, kb, IDIM), BF16),
                pltpu.VMEM((q, 2 * IDIM), BF16),
                pltpu.VMEM((q, 2 * IDIM), F32),
                pltpu.VMEM((2, 2 * q, window), F32),
                pltpu.VMEM((nh, 16, 128), BF16),
                pltpu.VMEM((nh, 16, 128), BF16),
                pltpu.VMEM((nh, 16, window // 4), BF16),
                pltpu.VMEM((nh, 16, window // 4), BF16),
                pltpu.VMEM((8 * nh, 128), F32),
                pltpu.VMEM((8 * nh, 128), F32),
                pltpu.VMEM((8 * nh, window), F32),
                pltpu.VMEM((8 * nh, window), BF16),
                pltpu.VMEM((8 * nh, window), BF16),
                pltpu.VMEM((8 * nh, 128), F32),
                pltpu.VMEM((nh, STEPS, per, 8, 128), F32),
                pltpu.VMEM((nh, STEPS, per, 8, 128), F32),
                pltpu.VMEM((nh, 16, 128), BF16),
                pltpu.VMEM((nh, 16, 128), BF16),
                pltpu.VMEM((STEPS, per, 8, 128), F32),
                pltpu.VMEM((STEPS - 1, per, 8, 128), F32),
                pltpu.VMEM((nh, per, 8, 128), F32),
                pltpu.VMEM((8 * nh, 128), F32),
                pltpu.VMEM((q, 128), F32),
                dma((7,)),
                dma((3,)),
                dma((3,)),
                dma((2,)),
                dma((2,)),
                dma((3,)),
                dma((3,)),
                dma((3,)),
                dma((3,)),
                dma((2,)),
                dma((2,)),
                dma((2,)),
                dma((2,)),
                dma((STEPS - 1,)),
                dma((STEPS - 1,)),
                dma((2,)),
            ],
            compiler_params=pltpu.CompilerParams(
                collective_id=0, has_side_effects=True, vmem_limit_bytes=48 << 20
            ),
        )(
            pltpu.with_memory_space_constraint(main_query, pltpu.MemorySpace.HBM),
            pltpu.with_memory_space_constraint(latent.T, pltpu.MemorySpace.HBM),
            main_outside.T,
            pltpu.with_memory_space_constraint(index_query, pltpu.MemorySpace.HBM),
            index_weights.T,
            pltpu.with_memory_space_constraint(index_keys, pltpu.MemorySpace.HBM),
            index_outside.reshape(1, q),
            query_pos.reshape(1, q),
            key_pos.reshape(1, kb),
        )
        return grad_query, grad_weight.T, grad_keys

    in_specs = (
        P("seq", "head"),
        P("seq", None),
        P("seq", "head"),
        P("seq", "head"),
        P("seq", "head"),
        P("seq", None),
        P("seq"),
        P("seq"),
        P("seq"),
    )
    out_specs = (P("seq", "head"), P("seq", "head"), P("seq", None))
    return jax.shard_map(shards, mesh=mesh, in_specs=in_specs, out_specs=out_specs, check_vma=False)
```

```python
import functools

import jax
import jax.numpy as jnp
from jax import lax
from jax.experimental import pallas as pl
from jax.experimental.pallas import tpu as pltpu
from jax.sharding import PartitionSpec as P

MESH = pl.DeviceIdType.MESH
STEPS = 4
IDIM = 128
WIDTH = 576
PAD = 64
WIDE = WIDTH + PAD
X_RUN = 4
X_ROWS = 320
Z_ROWS = WIDTH - X_ROWS
NEGATIVE = -1e30
ABSENT = 1e9
SCORE_SCALE = 192.0 ** (-0.5)
FACTOR = IDIM ** (-0.5)
F32 = jnp.float32
BF16 = jnp.bfloat16


def dot(a, b, dims):
    return lax.dot_general(a, b, (dims, ((), ())), preferred_element_type=F32)


def swap(x):
    return pltpu.roll(x, 4, 0)


def split_pair(a, b, low):
    return jnp.where(low, a, swap(b)), jnp.where(low, swap(a), b)


def high_part(x):
    return x.astype(BF16).astype(F32)


def kernel(
    ns,
    nh,
    main_query,
    latent,
    outside,
    index_query,
    index_weights,
    index_keys,
    index_outside,
    query_pos,
    key_pos,
    grad_query,
    grad_weight,
    grad_keys,
    rows,
    cols,
    place,
    queries,
    lat,
    keys,
    narrow_query,
    wide_query,
    scores,
    peaks,
    sums,
    index_score,
    dscores,
    ask_out,
    ask_in,
    mass_out,
    mass_in,
    near_query,
    near_weight,
    act,
    upper,
    lower,
    terms_out,
    terms_in,
    shared,
    back_out,
    back_in,
    part_out,
    part_in,
    final,
    weight_grad,
    local_sem,
    cross_send,
    cross_recv,
    direct_send,
    direct_recv,
    gather_send,
    gather_recv,
    forward_send,
    forward_recv,
    ask_sem,
    mass_sem,
    terms_sem,
    back_sem,
    shared_send,
    shared_recv,
    part_send,
    part_recv,
    final_sem,
):
    q_rows = index_query.shape[0]
    kb = key_pos.shape[1]
    window = STEPS * kb
    half = window // 2
    chunks = q_rows // 8
    blocks = kb // 128
    tiles = 16 * blocks
    per = tiles // nh
    head = lax.axis_index("head")
    seq = lax.axis_index("seq")

    local = []
    for parity in range(2):
        for i in range(2):
            start = (2 * i + parity) * WIDTH - parity * PAD
            local.append(
                pltpu.make_async_copy(
                    main_query.at[:, pl.ds(start, WIDE)],
                    queries.at[parity, pl.ds(i * q_rows, q_rows), :],
                    local_sem.at[2 * parity + i],
                )
            )
    local.append(
        pltpu.make_async_copy(latent, lat.at[STEPS - 1, pl.ds(PAD, WIDTH), :], local_sem.at[4])
    )
    local.append(pltpu.make_async_copy(index_keys, keys.at[STEPS - 1], local_sem.at[5]))
    local.append(pltpu.make_async_copy(index_query, narrow_query, local_sem.at[6]))
    for copy in local:
        copy.start()

    barrier = pltpu.get_barrier_semaphore()

    def greet(r, carry):
        pl.semaphore_signal(
            barrier, inc=1, device_id={"head": lax.rem(head + r, nh)}, device_id_type=MESH
        )
        return carry

    for distance in range(1, STEPS):
        for other in (seq + distance, seq + ns - distance):
            pl.semaphore_signal(
                barrier, inc=1, device_id={"seq": lax.rem(other, ns)}, device_id_type=MESH
            )
    lax.fori_loop(1, nh, greet, 0)

    pl.semaphore_wait(barrier, nh - 1 + 2 * (STEPS - 1))

    core = lax.rem(seq, 2)
    early, late = 2 * core, 2 - 2 * core
    ring, run = head // X_RUN, lax.rem(head, X_RUN)
    rings = nh // X_RUN
    run_rows, ring_rows, key_rows = X_ROWS // X_RUN, Z_ROWS // rings, kb // rings
    run_at = pl.multiple_of(run_rows * run, 16)
    ring_at = pl.multiple_of(X_ROWS + ring_rows * ring, 16)
    key_at = pl.multiple_of(key_rows * ring, 16)

    def lat_rows(slot, start, size):
        return lat.at[slot, pl.ds(pl.multiple_of(PAD + start, 16), size), :]

    def key_part(slot, start, size):
        return keys.at[slot, pl.ds(start, size), :]

    def to_seq(source, target, send, recv, i, other):
        return pltpu.make_async_remote_copy(
            src_ref=source,
            dst_ref=target,
            send_sem=send.at[i],
            recv_sem=recv.at[i],
            device_id={"seq": other},
            device_id_type=MESH,
        )

    two = lax.rem(seq + 2, ns)
    sibling = seq + 1 - 2 * core
    crossing = [
        to_seq(
            index_keys.at[pl.ds(key_at, key_rows), :],
            key_part(1, key_at, key_rows),
            cross_send, cross_recv, 0, two,
        ),
        to_seq(
            latent.at[pl.ds(ring_at, ring_rows), :],
            lat_rows(1, ring_at, ring_rows),
            cross_send, cross_recv, 1, two,
        ),
        to_seq(
            latent.at[pl.ds(run_at, run_rows), :],
            lat_rows(1, run_at, run_rows),
            cross_send, cross_recv, 2, two,
        ),
    ]
    onward = lax.rem(seq + 1 + 2 * core, ns)
    direct = [
        to_seq(index_keys, keys.at[late], direct_send, direct_recv, 0, onward),
        to_seq(latent, lat_rows(late, 0, WIDTH), direct_send, direct_recv, 1, onward),
    ]
    for copy in crossing + direct:
        copy.start()

    def exchange(source, target, sems, peer, slot):
        return pltpu.make_async_remote_copy(
            src_ref=source,
            dst_ref=target,
            send_sem=sems.at[0],
            recv_sem=sems.at[1],
            device_id={"head": peer},
            device_id_type=MESH,
        )

    def all_of(source, target, sems):
        return exchange(
            source.at[pl.ds(0, nh - 1)], target.at[pl.ds(0, nh - 1)], sems, lax.rem(head + 1, nh), 0
        )

    low = lax.broadcasted_iota(jnp.int32, (8, 128), 0) < 4
    lane = lax.broadcasted_iota(jnp.int32, (8, 128), 1)
    rows[...] = jnp.zeros_like(rows)
    rows[0:4, :] = outside[...]
    rows[4:6, :] = index_weights[...]
    rows[6:7, :] = query_pos[...].astype(F32)
    rows[7:8, :] = index_outside[...]
    cols[...] = rows[...].T
    for k in range(STEPS):
        here = jnp.where(seq >= STEPS - 1 - k, 0.0, ABSENT)
        own = key_pos[...].astype(F32) if k == STEPS - 1 else jnp.zeros((1, kb), F32)
        place[:, k * kb : (k + 1) * kb] = own + here
        lat[k, 0:PAD, :] = jnp.zeros((PAD, kb), BF16)
        lat[k, PAD + WIDTH : PAD + WIDTH + PAD, :] = jnp.zeros((PAD, kb), BF16)
    wide_lane = lax.broadcasted_iota(jnp.int32, (q_rows, 128), 1)
    for parity in range(2):
        for i in range(2):
            at = slice(i * q_rows, (i + 1) * q_rows)
            h = 2 * i + parity
            peaks[parity, at, :] = jnp.where(wide_lane == STEPS, cols[:, h : h + 1], NEGATIVE)
            sums[parity, at, :] = jnp.where(wide_lane == STEPS, 1.0, 0.0)
    local[6].wait()
    wide_query[...] = narrow_query[...].astype(F32)

    def ask(c, carry):
        at = pl.ds(pl.multiple_of(8 * c, 8), 8)
        values = wide_query[at, :]
        column = cols[at, :]
        first = jnp.broadcast_to(column[:, 4:5], (8, 128))
        second = jnp.broadcast_to(column[:, 5:6], (8, 128))
        pair = split_pair(values[:, :IDIM], values[:, IDIM:], low)
        weights = split_pair(first, second, low)
        for i in range(2):
            weight = weights[i]
            top = high_part(weight)
            mid = high_part(weight - top)
            end = weight - top - mid
            packed = jnp.where(lane == 0, top, jnp.where(lane == 1, mid, end))
            ask_out[2 * c + i] = jnp.concatenate([pair[i], packed], 0).astype(BF16)
        return carry

    lax.fori_loop(0, chunks, ask, 0)

    def send_ask(r, carry):
        peer = lax.rem(head + r, nh)
        exchange(ask_out.at[peer], ask_in.at[nh - 1 - r], ask_sem, peer, 0).start()
        return carry

    lax.fori_loop(1, nh, send_ask, 0)
    ask_in[nh - 1] = ask_out[head]

    def score_block(k):
        at = pl.ds(pl.multiple_of(k * kb, 128), kb)
        visible = place[:, at] <= cols[:, 6:7]
        for parity in range(2):
            table = lat[k, PAD * (1 - parity) : PAD * (1 - parity) + WIDE, :]
            x = dot(queries[parity], table, ((1,), (0,))) * SCORE_SCALE
            for i in range(2):
                own = slice(i * q_rows, (i + 1) * q_rows)
                masked = jnp.where(visible, x[own, :], NEGATIVE)
                peak = jnp.max(masked, axis=1, keepdims=True)
                e = jnp.exp(masked - peak)
                scores[parity, own, at] = e
                total = jnp.sum(e, axis=1, keepdims=True)
                peaks[parity, own, :] = jnp.where(wide_lane == k, peak, peaks[parity, own, :])
                sums[parity, own, :] = jnp.where(wide_lane == k, total, sums[parity, own, :])

    def act_block(k, asked):
        at = pl.ds(pl.multiple_of(k * kb, 128), kb)
        a = dot(asked, keys[k], ((1,), (1,))) * FACTOR
        act[:, at] = a
        weight = near_weight[...]
        weighed = jnp.concatenate([weight] * blocks, 1) * jnp.maximum(a, 0.0)
        index_score[:, at] = jnp.sum(weighed.reshape(nh, 8, kb), axis=0)

    def to_head(part, i, peer):
        return pltpu.make_async_remote_copy(
            src_ref=part,
            dst_ref=part,
            send_sem=gather_send.at[i],
            recv_sem=gather_recv.at[i],
            device_id={"head": peer},
            device_id_type=MESH,
        )

    for copy in local[:6]:
        copy.wait()
    score_block(STEPS - 1)
    for copy in crossing:
        copy.wait_recv()

    def push_ring(r, carry):
        peer = lax.rem(head + r * X_RUN, nh)
        to_head(key_part(1, key_at, key_rows), 0, peer).start()
        to_head(lat_rows(1, ring_at, ring_rows), 1, peer).start()
        return carry

    def push_run(r, carry):
        peer = ring * X_RUN + lax.rem(run + r, X_RUN)
        to_head(lat_rows(1, run_at, run_rows), 2, peer).start()
        return carry

    lax.fori_loop(1, rings, push_ring, 0)
    lax.fori_loop(1, X_RUN, push_run, 0)
    gathered = [
        to_head(key_part(1, 0, key_rows * (rings - 1)), 0, head),
        to_head(lat_rows(1, 0, ring_rows * (rings - 1)), 1, head),
        to_head(lat_rows(1, 0, run_rows * (X_RUN - 1)), 2, head),
    ]
    forward = [
        to_seq(keys.at[1], keys.at[early], forward_send, forward_recv, 0, sibling),
        to_seq(
            lat_rows(1, X_ROWS, Z_ROWS),
            lat_rows(early, X_ROWS, Z_ROWS),
            forward_send, forward_recv, 1, sibling,
        ),
        to_seq(
            lat_rows(1, 0, X_ROWS),
            lat_rows(early, 0, X_ROWS),
            forward_send, forward_recv, 2, sibling,
        ),
    ]
    for copy in direct:
        copy.wait_recv()
    score_block(early)
    for i in range(3):
        gathered[i].wait_recv()
        forward[i].start()
    score_block(1)


    forward[1].wait_recv()
    forward[2].wait_recv()
    score_block(late)

    for parity in range(2):
        peak = peaks[parity]
        share = jnp.exp(peak - jnp.max(peak, axis=1, keepdims=True))
        total = jnp.sum(share * sums[parity], axis=1, keepdims=True)
        peaks[parity] = share * (1.0 / total)

    def soften(step, carry):
        c = lax.rem(step + head // 2 + 1, chunks)
        parts = []
        for k in range(STEPS):
            part = jnp.zeros((8, kb), F32)
            for parity in range(2):
                for i in range(2):
                    own = pl.ds(pl.multiple_of(i * q_rows + 8 * c, 8), 8)
                    part = part + (
                        scores[parity, own, k * kb : (k + 1) * kb] * peaks[parity, own, k : k + 1]
                    )
            parts.append(part)
        mass = jnp.concatenate(parts, 1)
        halves = split_pair(
            mass[:, :half], mass[:, half:], lax.broadcasted_iota(jnp.int32, (8, half), 0) < 4
        )
        for i in range(2):
            peer = 2 * c + i
            mass_out[peer] = jnp.concatenate(
                [halves[i][:, : half // 2], halves[i][:, half // 2 :]], 0
            ).astype(BF16)

            @pl.when(peer != head)
            def _():
                r = lax.rem(peer + nh - head, nh)
                exchange(mass_out.at[peer], mass_in.at[nh - 1 - r], mass_sem, peer, 0).start()

        return carry

    lax.fori_loop(0, chunks, soften, 0)
    mass_in[nh - 1] = mass_out[head]

    all_of(ask_out, ask_in, ask_sem).wait_recv()

    both = ask_in[...].astype(F32)
    near_query[...] = both[:, 0:8, :].reshape(8 * nh, 128)
    packed = both[:, 8:16, :].reshape(8 * nh, 128)
    weight = packed[:, 0:1] + (packed[:, 1:2] + packed[:, 2:3])
    near_weight[...] = jnp.broadcast_to(weight, (8 * nh, 128))
    asked = near_query[...].astype(BF16)
    act_block(STEPS - 1, asked)
    act_block(early, asked)
    act_block(1, asked)
    forward[0].wait_recv()
    act_block(late, asked)

    score = index_score[...]
    score = score + swap(score)
    odd = lax.rem(head, 2)
    column = cols[pl.ds(pl.multiple_of(8 * (head // 2), 8), 8), :]
    pick = (lax.broadcasted_iota(jnp.int32, (8, 128), 0) // 4) == odd
    column = jnp.where(pick, column, swap(column))
    visible = place[...] <= column[:, 6:7]
    masked = jnp.where(visible, score, NEGATIVE)
    limit = column[:, 7:8]
    top = jnp.maximum(jnp.max(masked, axis=1, keepdims=True), limit)
    e = jnp.exp(masked - top)
    total = jnp.sum(e, axis=1, keepdims=True) + jnp.exp(limit - top)
    predicted = e * (1.0 / total)
    weighted = near_weight[...] * near_query[...]
    turned = weighted.T
    turned_high = turned.astype(BF16)
    turned_low = (turned - turned_high.astype(F32)).astype(BF16)

    all_of(mass_out, mass_in, mass_sem).wait_recv()
    mass = mass_in[0].astype(F32)
    for g in range(1, nh):
        mass = mass + mass_in[g].astype(F32)
    mass = jnp.concatenate([mass[0:8, :], mass[8:16, :]], 1)
    low_half = lax.broadcasted_iota(jnp.int32, (8, half), 0) < 4
    turned_mass = swap(mass)
    mass = jnp.concatenate(
        [jnp.where(low_half, mass, turned_mass), jnp.where(low_half, turned_mass, mass)], 1
    )
    target = mass * (1.0 / jnp.sum(mass, axis=1, keepdims=True))
    dscore = (predicted - target) * float(window)
    d_high = high_part(dscore)
    dscores[0] = d_high
    dscores[1] = dscore - d_high

    def term_block(k):
        at = pl.ds(pl.multiple_of(k * kb, 128), kb)
        on = act[:, at].reshape(nh, 8, kb) > 0.0
        gated = []
        for i in range(2):
            chosen = jnp.where(on, dscores[i, :, at][None], 0.0)
            gated.append(chosen.reshape(8 * nh, kb).astype(BF16))
        upper[:, at] = gated[0]
        lower[:, at] = gated[1]
        terms = dot(turned_high, gated[0], ((1,), (0,)))
        terms = terms + dot(turned_low, gated[0], ((1,), (0,)))
        terms = terms + dot(turned_high, gated[1], ((1,), (0,)))
        terms = terms * FACTOR
        for tile in range(tiles):
            d, b = tile // blocks, tile % blocks
            terms_out[k, tile // per, tile % per] = terms[
                8 * d : 8 * d + 8, 128 * b : 128 * b + 128
            ]

    term_block(3 - 3 * core)
    share_first = to_seq(
        terms_out.at[3 - 3 * core], shared.at[0], shared_send, shared_recv, 0, sibling
    )
    share_second = to_seq(terms_out.at[1], shared.at[1], shared_send, shared_recv, 1, sibling)
    share_first.start()
    term_block(core)

    @pl.when(core == 1)
    def _():
        share_second.start()

    term_block(1 + core)
    term_block(2 + core)
    share_first.wait_recv()

    @pl.when(core == 0)
    def _():
        share_second.wait_recv()
        terms_out[1] = terms_out[1] + shared[0]
        terms_out[2] = terms_out[2] + shared[1]

    @pl.when(core == 1)
    def _():
        terms_out[2] = terms_out[2] + shared[0]

    def terms_to(first, count, peer, slot):
        return exchange(
            terms_out.at[pl.ds(first, count), peer],
            terms_in.at[pl.ds(first, count), slot],
            terms_sem, peer, 0,
        )

    def terms_all(first, count):
        return exchange(
            terms_out.at[pl.ds(first, count), pl.ds(0, nh - 1)],
            terms_in.at[pl.ds(first, count), pl.ds(0, nh - 1)],
            terms_sem, lax.rem(head + 1, nh), 0,
        )

    def send_terms(first, count):
        def send(r, carry):
            terms_to(first, count, lax.rem(head + r, nh), nh - 1 - r).start()
            return carry

        lax.fori_loop(1, nh, send, 0)

    @pl.when(core == 0)
    def _():
        send_terms(0, 3)

    @pl.when(core == 1)
    def _():
        send_terms(2, 2)

    all_keys = keys[...].reshape(window, IDIM)
    near_grad = dot(upper[...], all_keys, ((1,), (0,))) + dot(lower[...], all_keys, ((1,), (0,)))
    near_grad = near_grad * FACTOR * near_weight[...]

    share = jnp.zeros((8 * nh, 1), F32)
    for k in range(STEPS):
        at = slice(k * kb, (k + 1) * kb)
        rectified = jnp.maximum(act[:, at], 0.0).reshape(nh, 8, kb)
        product = (rectified * dscore[:, at][None]).reshape(8 * nh, kb)
        share = share + jnp.sum(product, axis=1, keepdims=True)
    tall_lane = lax.broadcasted_iota(jnp.int32, (8 * nh, 128), 1)
    top = high_part(share)
    mid = high_part(share - top)
    packed = jnp.where(tall_lane == 0, top, jnp.where(tall_lane == 1, mid, share - top - mid))
    back_out[...] = jnp.concatenate(
        [near_grad.reshape(nh, 8, 128), packed.reshape(nh, 8, 128)], 1
    ).astype(BF16)

    def sum_terms(k):
        total = terms_out[k, head]
        for g in range(nh - 1):
            total = total + terms_in[k, g]
        part_out[k] = total

    behind = lax.rem(seq + ns - 2, ns)

    def part(k, slot, other):
        return pltpu.make_async_remote_copy(
            src_ref=part_out.at[k],
            dst_ref=part_in.at[slot],
            send_sem=part_send.at[k],
            recv_sem=part_recv.at[slot],
            device_id={"seq": other},
            device_id_type=MESH,
        )

    part_even = [
        part(1, 1, behind),
        part(2, 0, lax.rem(seq + ns - 1, ns)),
        part(0, 1, lax.rem(seq + ns - 3, ns)),
    ]
    part_odd = part(2, 0, sibling)

    @pl.when(core == 0)
    def _():
        terms_all(0, 3).wait_recv()
        for k in (1, 2, 0):
            sum_terms(k)
        for copy in part_even:
            copy.start()

    @pl.when(core == 1)
    def _():
        terms_all(2, 2).wait_recv()
        for k in (2, 3):
            sum_terms(k)
        part_odd.start()

    def send_back(r, carry):
        peer = lax.rem(head + r, nh)
        exchange(back_out.at[r - 1], back_in.at[head], back_sem, peer, 0).start()
        return carry

    lax.fori_loop(1, nh, send_back, 0)
    back_in[head] = back_out[nh - 1]

    part(1, 0, behind).wait_recv()
    part(1, 1, behind).wait_recv()
    mine = jnp.where(core == 1, part_out[3], 0.0) + part_in[0] + part_in[1]
    final[head] = mine

    def send_final(r, carry):
        peer = lax.rem(head + r, nh)
        exchange(final.at[head], final.at[head], final_sem, peer, 0).start()
        return carry

    lax.fori_loop(1, nh, send_final, 0)

    all_of(back_out, back_in, back_sem).wait_recv()

    def unpack_back(c, carry):
        at = pl.ds(pl.multiple_of(8 * c, 8), 8)
        one = back_in[2 * c].astype(F32)
        two = back_in[2 * c + 1].astype(F32)
        first, second = split_pair(one[0:8, :], two[0:8, :], low)
        wide_query[at, 0:IDIM] = first
        wide_query[at, IDIM : 2 * IDIM] = second
        shares = []
        for packed in (one[8:16, :], two[8:16, :]):
            share = packed[:, 0:1] + (packed[:, 1:2] + packed[:, 2:3])
            shares.append(jnp.broadcast_to(share, (8, 128)))
        first, second = split_pair(shares[0], shares[1], low)
        weight_grad[at, :] = jnp.where(lane == 0, first, second)
        return carry

    lax.fori_loop(0, chunks, unpack_back, 0)
    grad_query[...] = wide_query[...].astype(BF16)
    grad_weight[...] = weight_grad[...].T[0:2, :]

    all_of(final, final, final_sem).wait_recv()
    for b in range(blocks):
        columns = [final[(d * blocks + b) // per, (d * blocks + b) % per] for d in range(16)]
        grad_keys[128 * b : 128 * b + 128, :] = jnp.concatenate(columns, 0).T

    for copy in crossing + direct + gathered + forward + [share_first]:
        copy.wait_send()

    @pl.when(core == 0)
    def _():
        terms_all(0, 3).wait_send()
        for copy in part_even:
            copy.wait_send()

    @pl.when(core == 1)
    def _():
        share_second.wait_send()
        terms_all(2, 2).wait_send()
        part_odd.wait_send()

    all_of(ask_out, ask_in, ask_sem).wait_send()
    all_of(mass_out, mass_in, mass_sem).wait_send()
    all_of(back_out, back_in, back_sem).wait_send()
    all_of(final, final, final_sem).wait_send()


def solution(mesh):
    ns, nh = mesh.shape["seq"], mesh.shape["head"]

    def shards(
        main_query,
        latent,
        main_outside,
        index_query,
        index_weights,
        index_keys,
        index_outside,
        query_pos,
        key_pos,
    ):
        q = main_query.shape[0]
        kb = latent.shape[0]
        window = STEPS * kb
        per = 16 * (kb // 128) // nh
        vmem = pl.BlockSpec(memory_space=pltpu.VMEM)
        whole = pl.BlockSpec(memory_space=pltpu.MemorySpace.HBM)
        dma = pltpu.SemaphoreType.DMA
        grad_query, grad_weight, grad_keys = pl.pallas_call(
            functools.partial(kernel, ns, nh),
            out_shape=(
                jax.ShapeDtypeStruct((q, 2 * IDIM), BF16),
                jax.ShapeDtypeStruct((2, q), F32),
                jax.ShapeDtypeStruct((kb, IDIM), F32),
            ),
            in_specs=[whole, whole, vmem, whole, vmem, whole, vmem, vmem, vmem],
            out_specs=(vmem, vmem, vmem),
            scratch_shapes=[
                pltpu.VMEM((128, q), F32),
                pltpu.VMEM((q, 128), F32),
                pltpu.VMEM((1, window), F32),
                pltpu.VMEM((2, 2 * q, WIDE), BF16),
                pltpu.VMEM((STEPS, WIDE + PAD, kb), BF16),
                pltpu.VMEM((STEPS, kb, IDIM), BF16),
                pltpu.VMEM((q, 2 * IDIM), BF16),
                pltpu.VMEM((q, 2 * IDIM), F32),
                pltpu.VMEM((2, 2 * q, window), F32),
                pltpu.VMEM((2, 2 * q, 128), F32),
                pltpu.VMEM((2, 2 * q, 128), F32),
                pltpu.VMEM((8, window), F32),
                pltpu.VMEM((2, 8, window), F32),
                pltpu.VMEM((nh, 16, 128), BF16),
                pltpu.VMEM((nh, 16, 128), BF16),
                pltpu.VMEM((nh, 16, window // 4), BF16),
                pltpu.VMEM((nh, 16, window // 4), BF16),
                pltpu.VMEM((8 * nh, 128), F32),
                pltpu.VMEM((8 * nh, 128), F32),
                pltpu.VMEM((8 * nh, window), F32),
                pltpu.VMEM((8 * nh, window), BF16),
                pltpu.VMEM((8 * nh, window), BF16),
                pltpu.VMEM((STEPS, nh, per, 8, 128), F32),
                pltpu.VMEM((STEPS, nh, per, 8, 128), F32),
                pltpu.VMEM((2, nh, per, 8, 128), F32),
                pltpu.VMEM((nh, 16, 128), BF16),
                pltpu.VMEM((nh, 16, 128), BF16),
                pltpu.VMEM((STEPS, per, 8, 128), F32),
                pltpu.VMEM((2, per, 8, 128), F32),
                pltpu.VMEM((nh, per, 8, 128), F32),
                pltpu.VMEM((q, 128), F32),
                dma((7,)),
                dma((3,)),
                dma((3,)),
                dma((2,)),
                dma((2,)),
                dma((3,)),
                dma((3,)),
                dma((3,)),
                dma((3,)),
                dma((2,)),
                dma((2,)),
                dma((2,)),
                dma((2,)),
                dma((2,)),
                dma((2,)),
                dma((STEPS - 1,)),
                dma((2,)),
                dma((2,)),
            ],
            compiler_params=pltpu.CompilerParams(
                collective_id=0, has_side_effects=True, vmem_limit_bytes=48 << 20
            ),
        )(
            pltpu.with_memory_space_constraint(main_query, pltpu.MemorySpace.HBM),
            pltpu.with_memory_space_constraint(latent.T, pltpu.MemorySpace.HBM),
            main_outside.T,
            pltpu.with_memory_space_constraint(index_query, pltpu.MemorySpace.HBM),
            index_weights.T,
            pltpu.with_memory_space_constraint(index_keys, pltpu.MemorySpace.HBM),
            index_outside.reshape(1, q),
            query_pos.reshape(1, q),
            key_pos.reshape(1, kb),
        )
        return grad_query, grad_weight.T, grad_keys

    in_specs = (
        P("seq", "head"),
        P("seq", None),
        P("seq", "head"),
        P("seq", "head"),
        P("seq", "head"),
        P("seq", None),
        P("seq"),
        P("seq"),
        P("seq"),
    )
    out_specs = (P("seq", "head"), P("seq", "head"), P("seq", None))
    return jax.shard_map(shards, mesh=mesh, in_specs=in_specs, out_specs=out_specs, check_vma=False)
```

```python
import functools

import jax
import jax.numpy as jnp
from jax import lax
from jax.experimental import pallas as pl
from jax.experimental.pallas import tpu as pltpu
from jax.sharding import PartitionSpec as P

MESH = pl.DeviceIdType.MESH
STEPS = 4
IDIM = 128
WIDTH = 576
PAD = 64
WIDE = WIDTH + PAD
X_RUN = 4
X_ROWS = 320
Z_ROWS = WIDTH - X_ROWS
NEGATIVE = -1e30
ABSENT = 1e9
SCORE_SCALE = 192.0 ** (-0.5)
FACTOR = IDIM ** (-0.5)
F32 = jnp.float32
BF16 = jnp.bfloat16


def dot(a, b, dims):
    return lax.dot_general(a, b, (dims, ((), ())), preferred_element_type=F32)


def swap(x):
    return pltpu.roll(x, 4, 0)


def split_pair(a, b, low):
    return jnp.where(low, a, swap(b)), jnp.where(low, swap(a), b)


def high_part(x):
    return x.astype(BF16).astype(F32)


def kernel(
    ns,
    nh,
    main_query,
    latent,
    far_outside,
    index_query,
    far_weights,
    index_keys,
    far_limit,
    far_query_pos,
    far_key_pos,
    grad_query,
    grad_weight,
    grad_keys,
    outside,
    index_weights,
    index_outside,
    query_pos,
    key_pos,
    rows,
    cols,
    place,
    queries,
    lat,
    keys,
    narrow_query,
    wide_query,
    scores,
    peaks,
    sums,
    index_score,
    dscores,
    ask_out,
    ask_in,
    mass_out,
    mass_in,
    near_query,
    near_weight,
    act,
    upper,
    lower,
    terms_out,
    terms_in,
    shared,
    back_out,
    back_in,
    part_out,
    part_in,
    final,
    weight_grad,
    small_sem,
    local_sem,
    cross_send,
    cross_recv,
    direct_send,
    direct_recv,
    gather_send,
    gather_recv,
    forward_send,
    forward_recv,
    ask_sem,
    mass_sem,
    terms_sem,
    alone_sem,
    back_sem,
    shared_send,
    shared_recv,
    part_send,
    part_recv,
    final_sem,
):
    q_rows = index_query.shape[0]
    kb = key_pos.shape[1]
    window = STEPS * kb
    half = window // 2
    chunks = q_rows // 8
    blocks = kb // 128
    tiles = 16 * blocks
    per = tiles // nh
    head = lax.axis_index("head")
    seq = lax.axis_index("seq")

    local = []
    for parity in range(2):
        for i in range(2):
            start = (2 * i + parity) * WIDTH - parity * PAD
            local.append(
                pltpu.make_async_copy(
                    main_query.at[:, pl.ds(start, WIDE)],
                    queries.at[parity, pl.ds(i * q_rows, q_rows), :],
                    local_sem.at[2 * parity + i],
                )
            )
    local.append(
        pltpu.make_async_copy(latent, lat.at[STEPS - 1, pl.ds(PAD, WIDTH), :], local_sem.at[4])
    )
    local.append(pltpu.make_async_copy(index_keys, keys.at[STEPS - 1], local_sem.at[5]))
    local.append(pltpu.make_async_copy(index_query, narrow_query, local_sem.at[6]))
    small = [
        pltpu.make_async_copy(source, target, small_sem.at[i])
        for i, (source, target) in enumerate(
            (
                (far_outside, outside),
                (far_weights, index_weights),
                (far_limit, index_outside),
                (far_query_pos, query_pos),
                (far_key_pos, key_pos),
            )
        )
    ]
    for copy in small + local[6:] + local[:6]:
        copy.start()

    barrier = pltpu.get_barrier_semaphore()

    def greet(r, carry):
        pl.semaphore_signal(
            barrier, inc=1, device_id={"head": lax.rem(head + r, nh)}, device_id_type=MESH
        )
        return carry

    for distance in range(1, STEPS):
        for other in (seq + distance, seq + ns - distance):
            pl.semaphore_signal(
                barrier, inc=1, device_id={"seq": lax.rem(other, ns)}, device_id_type=MESH
            )
    lax.fori_loop(1, nh, greet, 0)

    pl.semaphore_wait(barrier, nh - 1 + 2 * (STEPS - 1))

    core = lax.rem(seq, 2)
    early, late = 2 * core, 2 - 2 * core
    ring, run = head // X_RUN, lax.rem(head, X_RUN)
    rings = nh // X_RUN
    run_rows, ring_rows, key_rows = X_ROWS // X_RUN, Z_ROWS // rings, kb // rings
    run_at = pl.multiple_of(run_rows * run, 16)
    ring_at = pl.multiple_of(X_ROWS + ring_rows * ring, 16)
    key_at = pl.multiple_of(key_rows * ring, 16)

    def lat_rows(slot, start, size):
        return lat.at[slot, pl.ds(pl.multiple_of(PAD + start, 16), size), :]

    def key_part(slot, start, size):
        return keys.at[slot, pl.ds(start, size), :]

    def to_seq(source, target, send, recv, i, other):
        return pltpu.make_async_remote_copy(
            src_ref=source,
            dst_ref=target,
            send_sem=send.at[i],
            recv_sem=recv.at[i],
            device_id={"seq": other},
            device_id_type=MESH,
        )

    two = lax.rem(seq + 2, ns)
    sibling = seq + 1 - 2 * core
    crossing = [
        to_seq(
            index_keys.at[pl.ds(key_at, key_rows), :],
            key_part(1, key_at, key_rows),
            cross_send, cross_recv, 0, two,
        ),
        to_seq(
            latent.at[pl.ds(ring_at, ring_rows), :],
            lat_rows(1, ring_at, ring_rows),
            cross_send, cross_recv, 1, two,
        ),
        to_seq(
            latent.at[pl.ds(run_at, run_rows), :],
            lat_rows(1, run_at, run_rows),
            cross_send, cross_recv, 2, two,
        ),
    ]
    onward = lax.rem(seq + 1 + 2 * core, ns)
    direct = [
        to_seq(index_keys, keys.at[late], direct_send, direct_recv, 0, onward),
        to_seq(latent, lat_rows(late, 0, WIDTH), direct_send, direct_recv, 1, onward),
    ]
    for copy in crossing[::-1] + direct[::-1]:
        copy.start()

    def exchange(source, target, sems, peer, slot):
        return pltpu.make_async_remote_copy(
            src_ref=source,
            dst_ref=target,
            send_sem=sems.at[0],
            recv_sem=sems.at[1],
            device_id={"head": peer},
            device_id_type=MESH,
        )

    def all_of(source, target, sems):
        return exchange(
            source.at[pl.ds(0, nh - 1)], target.at[pl.ds(0, nh - 1)], sems, lax.rem(head + 1, nh), 0
        )

    low = lax.broadcasted_iota(jnp.int32, (8, 128), 0) < 4
    lane = lax.broadcasted_iota(jnp.int32, (8, 128), 1)
    for copy in small:
        copy.wait()
    rows[...] = jnp.zeros_like(rows)
    rows[0:4, :] = outside[...]
    rows[4:6, :] = index_weights[...]
    rows[6:7, :] = query_pos[...].astype(F32)
    rows[7:8, :] = index_outside[...]
    cols[...] = rows[...].T
    for k in range(STEPS):
        here = jnp.where(seq >= STEPS - 1 - k, 0.0, ABSENT)
        own = key_pos[...].astype(F32) if k == STEPS - 1 else jnp.zeros((1, kb), F32)
        place[:, k * kb : (k + 1) * kb] = own + here
        lat[k, 0:PAD, :] = jnp.zeros((PAD, kb), BF16)
        lat[k, PAD + WIDTH : PAD + WIDTH + PAD, :] = jnp.zeros((PAD, kb), BF16)
    wide_lane = lax.broadcasted_iota(jnp.int32, (q_rows, 128), 1)
    for parity in range(2):
        for i in range(2):
            at = slice(i * q_rows, (i + 1) * q_rows)
            h = 2 * i + parity
            peaks[parity, at, :] = jnp.where(wide_lane == STEPS, cols[:, h : h + 1], NEGATIVE)
            sums[parity, at, :] = jnp.where(wide_lane == STEPS, 1.0, 0.0)
    local[6].wait()
    wide_query[...] = narrow_query[...].astype(F32)

    def ask(c, carry):
        at = pl.ds(pl.multiple_of(8 * c, 8), 8)
        values = wide_query[at, :]
        column = cols[at, :]
        first = jnp.broadcast_to(column[:, 4:5], (8, 128))
        second = jnp.broadcast_to(column[:, 5:6], (8, 128))
        pair = split_pair(values[:, :IDIM], values[:, IDIM:], low)
        weights = split_pair(first, second, low)
        for i in range(2):
            weight = weights[i]
            top = high_part(weight)
            mid = high_part(weight - top)
            end = weight - top - mid
            packed = jnp.where(lane == 0, top, jnp.where(lane == 1, mid, end))
            ask_out[2 * c + i] = jnp.concatenate([pair[i], packed], 0).astype(BF16)
        return carry

    lax.fori_loop(0, chunks, ask, 0)

    def send_ask(r, carry):
        peer = lax.rem(head + r, nh)
        exchange(ask_out.at[peer], ask_in.at[nh - 1 - r], ask_sem, peer, 0).start()
        return carry

    lax.fori_loop(1, nh, send_ask, 0)
    ask_in[nh - 1] = ask_out[head]

    def score_block(k):
        at = pl.ds(pl.multiple_of(k * kb, 128), kb)
        visible = place[:, at] <= cols[:, 6:7]
        for parity in range(2):
            table = lat[k, PAD * (1 - parity) : PAD * (1 - parity) + WIDE, :]
            x = dot(queries[parity], table, ((1,), (0,))) * SCORE_SCALE
            for i in range(2):
                own = slice(i * q_rows, (i + 1) * q_rows)
                masked = jnp.where(visible, x[own, :], NEGATIVE)
                peak = jnp.max(masked, axis=1, keepdims=True)
                e = jnp.exp(masked - peak)
                scores[parity, own, at] = e
                total = jnp.sum(e, axis=1, keepdims=True)
                peaks[parity, own, :] = jnp.where(wide_lane == k, peak, peaks[parity, own, :])
                sums[parity, own, :] = jnp.where(wide_lane == k, total, sums[parity, own, :])

    def act_block(k, asked):
        at = pl.ds(pl.multiple_of(k * kb, 128), kb)
        a = dot(asked, keys[k], ((1,), (1,))) * FACTOR
        act[:, at] = a
        weight = near_weight[...]
        weighed = jnp.concatenate([weight] * blocks, 1) * jnp.maximum(a, 0.0)
        index_score[:, at] = jnp.sum(weighed.reshape(nh, 8, kb), axis=0)

    def to_head(part, i, peer):
        return pltpu.make_async_remote_copy(
            src_ref=part,
            dst_ref=part,
            send_sem=gather_send.at[i],
            recv_sem=gather_recv.at[i],
            device_id={"head": peer},
            device_id_type=MESH,
        )

    for copy in local[:6]:
        copy.wait()
    score_block(STEPS - 1)
    def push_run(r, carry):
        peer = ring * X_RUN + lax.rem(run + r, X_RUN)
        to_head(lat_rows(1, run_at, run_rows), 2, peer).start()
        return carry

    def push_ring(r, carry):
        peer = lax.rem(head + r * X_RUN, nh)
        to_head(lat_rows(1, ring_at, ring_rows), 1, peer).start()
        return carry

    def push_keys(r, carry):
        peer = lax.rem(head + r * X_RUN, nh)
        to_head(key_part(1, key_at, key_rows), 0, peer).start()
        return carry

    crossing[2].wait_recv()
    lax.fori_loop(1, X_RUN, push_run, 0)
    crossing[1].wait_recv()
    lax.fori_loop(1, rings, push_ring, 0)
    crossing[0].wait_recv()
    lax.fori_loop(1, rings, push_keys, 0)
    gathered = [
        to_head(key_part(1, 0, key_rows * (rings - 1)), 0, head),
        to_head(lat_rows(1, 0, ring_rows * (rings - 1)), 1, head),
        to_head(lat_rows(1, 0, run_rows * (X_RUN - 1)), 2, head),
    ]
    forward = [
        to_seq(keys.at[1], keys.at[early], forward_send, forward_recv, 0, sibling),
        to_seq(
            lat_rows(1, X_ROWS, Z_ROWS),
            lat_rows(early, X_ROWS, Z_ROWS),
            forward_send, forward_recv, 1, sibling,
        ),
        to_seq(
            lat_rows(1, 0, X_ROWS),
            lat_rows(early, 0, X_ROWS),
            forward_send, forward_recv, 2, sibling,
        ),
    ]
    for copy in direct:
        copy.wait_recv()
    score_block(early)
    for i in (2, 1):
        gathered[i].wait_recv()
        forward[i].start()
    score_block(1)
    gathered[0].wait_recv()
    forward[0].start()


    forward[1].wait_recv()
    forward[2].wait_recv()
    score_block(late)

    for parity in range(2):
        peak = peaks[parity]
        share = jnp.exp(peak - jnp.max(peak, axis=1, keepdims=True))
        total = jnp.sum(share * sums[parity], axis=1, keepdims=True)
        peaks[parity] = share * (1.0 / total)

    def soften(step, carry):
        c = lax.rem(step + head // 2 + 1, chunks)
        parts = []
        for k in range(STEPS):
            part = jnp.zeros((8, kb), F32)
            for parity in range(2):
                for i in range(2):
                    own = pl.ds(pl.multiple_of(i * q_rows + 8 * c, 8), 8)
                    part = part + (
                        scores[parity, own, k * kb : (k + 1) * kb] * peaks[parity, own, k : k + 1]
                    )
            parts.append(part)
        mass = jnp.concatenate(parts, 1)
        halves = split_pair(
            mass[:, :half], mass[:, half:], lax.broadcasted_iota(jnp.int32, (8, half), 0) < 4
        )
        for i in range(2):
            peer = 2 * c + i
            mass_out[peer] = jnp.concatenate(
                [halves[i][:, : half // 2], halves[i][:, half // 2 :]], 0
            ).astype(BF16)

            @pl.when(peer != head)
            def _():
                r = lax.rem(peer + nh - head, nh)
                exchange(mass_out.at[peer], mass_in.at[nh - 1 - r], mass_sem, peer, 0).start()

        return carry

    lax.fori_loop(0, chunks, soften, 0)
    mass_in[nh - 1] = mass_out[head]

    all_of(ask_out, ask_in, ask_sem).wait_recv()

    both = ask_in[...].astype(F32)
    near_query[...] = both[:, 0:8, :].reshape(8 * nh, 128)
    packed = both[:, 8:16, :].reshape(8 * nh, 128)
    weight = packed[:, 0:1] + (packed[:, 1:2] + packed[:, 2:3])
    near_weight[...] = jnp.broadcast_to(weight, (8 * nh, 128))
    asked = near_query[...].astype(BF16)
    act_block(STEPS - 1, asked)
    act_block(early, asked)
    act_block(1, asked)
    forward[0].wait_recv()
    act_block(late, asked)

    score = index_score[...]
    score = score + swap(score)
    odd = lax.rem(head, 2)
    column = cols[pl.ds(pl.multiple_of(8 * (head // 2), 8), 8), :]
    pick = (lax.broadcasted_iota(jnp.int32, (8, 128), 0) // 4) == odd
    column = jnp.where(pick, column, swap(column))
    visible = place[...] <= column[:, 6:7]
    masked = jnp.where(visible, score, NEGATIVE)
    limit = column[:, 7:8]
    top = jnp.maximum(jnp.max(masked, axis=1, keepdims=True), limit)
    e = jnp.exp(masked - top)
    total = jnp.sum(e, axis=1, keepdims=True) + jnp.exp(limit - top)
    predicted = e * (1.0 / total)
    weighted = near_weight[...] * near_query[...]
    turned = weighted.T
    turned_high = turned.astype(BF16)
    turned_low = (turned - turned_high.astype(F32)).astype(BF16)

    all_of(mass_out, mass_in, mass_sem).wait_recv()
    mass = mass_in[0].astype(F32)
    for g in range(1, nh):
        mass = mass + mass_in[g].astype(F32)
    mass = jnp.concatenate([mass[0:8, :], mass[8:16, :]], 1)
    low_half = lax.broadcasted_iota(jnp.int32, (8, half), 0) < 4
    turned_mass = swap(mass)
    mass = jnp.concatenate(
        [jnp.where(low_half, mass, turned_mass), jnp.where(low_half, turned_mass, mass)], 1
    )
    target = mass * (1.0 / jnp.sum(mass, axis=1, keepdims=True))
    dscore = (predicted - target) * float(window)
    d_high = high_part(dscore)
    dscores[0] = d_high
    dscores[1] = dscore - d_high

    def term_block(k):
        at = pl.ds(pl.multiple_of(k * kb, 128), kb)
        on = act[:, at].reshape(nh, 8, kb) > 0.0
        gated = []
        for i in range(2):
            chosen = jnp.where(on, dscores[i, :, at][None], 0.0)
            gated.append(chosen.reshape(8 * nh, kb).astype(BF16))
        upper[:, at] = gated[0]
        lower[:, at] = gated[1]
        terms = dot(turned_high, gated[0], ((1,), (0,)))
        terms = terms + dot(turned_low, gated[0], ((1,), (0,)))
        terms = terms + dot(turned_high, gated[1], ((1,), (0,)))
        terms = terms * FACTOR
        for tile in range(tiles):
            d, b = tile // blocks, tile % blocks
            terms_out[k, tile // per, tile % per] = terms[
                8 * d : 8 * d + 8, 128 * b : 128 * b + 128
            ]

    def terms_to(first, count, peer, slot, sems):
        return exchange(
            terms_out.at[pl.ds(first, count), peer],
            terms_in.at[pl.ds(first, count), slot],
            sems, peer, 0,
        )

    def terms_all(first, count, sems):
        return exchange(
            terms_out.at[pl.ds(first, count), pl.ds(0, nh - 1)],
            terms_in.at[pl.ds(first, count), pl.ds(0, nh - 1)],
            sems, lax.rem(head + 1, nh), 0,
        )

    def send_terms(first, count, sems):
        def send(r, carry):
            terms_to(first, count, lax.rem(head + r, nh), nh - 1 - r, sems).start()
            return carry

        lax.fori_loop(1, nh, send, 0)

    term_block(3 - 3 * core)
    share_first = to_seq(
        terms_out.at[3 - 3 * core], shared.at[0], shared_send, shared_recv, 0, sibling
    )
    share_second = to_seq(terms_out.at[1], shared.at[1], shared_send, shared_recv, 1, sibling)
    share_first.start()
    term_block(core)

    @pl.when(core == 1)
    def _():
        share_second.start()

    term_block(1 + 2 * core)
    send_terms(3 * core, 1, alone_sem)
    term_block(2)
    share_first.wait_recv()

    @pl.when(core == 0)
    def _():
        share_second.wait_recv()
        terms_out[1] = terms_out[1] + shared[0]
        terms_out[2] = terms_out[2] + shared[1]
        send_terms(1, 2, terms_sem)

    @pl.when(core == 1)
    def _():
        terms_out[2] = terms_out[2] + shared[0]
        send_terms(2, 1, terms_sem)

    all_keys = keys[...].reshape(window, IDIM)
    near_grad = dot(upper[...], all_keys, ((1,), (0,))) + dot(lower[...], all_keys, ((1,), (0,)))
    near_grad = near_grad * FACTOR * near_weight[...]

    share = jnp.zeros((8 * nh, 1), F32)
    for k in range(STEPS):
        at = slice(k * kb, (k + 1) * kb)
        rectified = jnp.maximum(act[:, at], 0.0).reshape(nh, 8, kb)
        product = (rectified * dscore[:, at][None]).reshape(8 * nh, kb)
        share = share + jnp.sum(product, axis=1, keepdims=True)
    tall_lane = lax.broadcasted_iota(jnp.int32, (8 * nh, 128), 1)
    top = high_part(share)
    mid = high_part(share - top)
    packed = jnp.where(tall_lane == 0, top, jnp.where(tall_lane == 1, mid, share - top - mid))
    back_out[...] = jnp.concatenate(
        [near_grad.reshape(nh, 8, 128), packed.reshape(nh, 8, 128)], 1
    ).astype(BF16)

    def sum_terms(k):
        total = terms_out[k, head]
        for g in range(nh - 1):
            total = total + terms_in[k, g]
        part_out[k] = total

    behind = lax.rem(seq + ns - 2, ns)

    def part(k, slot, other):
        return pltpu.make_async_remote_copy(
            src_ref=part_out.at[k],
            dst_ref=part_in.at[slot],
            send_sem=part_send.at[k],
            recv_sem=part_recv.at[slot],
            device_id={"seq": other},
            device_id_type=MESH,
        )

    part_even = [
        part(1, 1, behind),
        part(2, 0, lax.rem(seq + ns - 1, ns)),
        part(0, 1, lax.rem(seq + ns - 3, ns)),
    ]
    part_odd = part(2, 0, sibling)

    @pl.when(core == 0)
    def _():
        terms_all(0, 1, alone_sem).wait_recv()
        sum_terms(0)
        terms_all(1, 2, terms_sem).wait_recv()
        for k in (1, 2):
            sum_terms(k)
        for copy in part_even:
            copy.start()

    @pl.when(core == 1)
    def _():
        terms_all(3, 1, alone_sem).wait_recv()
        sum_terms(3)
        terms_all(2, 1, terms_sem).wait_recv()
        sum_terms(2)
        part_odd.start()

    def send_back(r, carry):
        peer = lax.rem(head + r, nh)
        exchange(back_out.at[r - 1], back_in.at[head], back_sem, peer, 0).start()
        return carry

    lax.fori_loop(1, nh, send_back, 0)
    back_in[head] = back_out[nh - 1]

    part(1, 0, behind).wait_recv()
    part(1, 1, behind).wait_recv()
    mine = jnp.where(core == 1, part_out[3], 0.0) + part_in[0] + part_in[1]
    final[head] = mine

    def send_final(r, carry):
        peer = lax.rem(head + r, nh)
        exchange(final.at[head], final.at[head], final_sem, peer, 0).start()
        return carry

    lax.fori_loop(1, nh, send_final, 0)

    all_of(back_out, back_in, back_sem).wait_recv()

    def unpack_back(c, carry):
        at = pl.ds(pl.multiple_of(8 * c, 8), 8)
        one = back_in[2 * c].astype(F32)
        two = back_in[2 * c + 1].astype(F32)
        first, second = split_pair(one[0:8, :], two[0:8, :], low)
        wide_query[at, 0:IDIM] = first
        wide_query[at, IDIM : 2 * IDIM] = second
        shares = []
        for packed in (one[8:16, :], two[8:16, :]):
            share = packed[:, 0:1] + (packed[:, 1:2] + packed[:, 2:3])
            shares.append(jnp.broadcast_to(share, (8, 128)))
        first, second = split_pair(shares[0], shares[1], low)
        weight_grad[at, :] = jnp.where(lane == 0, first, second)
        return carry

    lax.fori_loop(0, chunks, unpack_back, 0)
    grad_query[...] = wide_query[...].astype(BF16)
    grad_weight[...] = weight_grad[...].T[0:2, :]

    all_of(final, final, final_sem).wait_recv()
    for b in range(blocks):
        columns = [final[(d * blocks + b) // per, (d * blocks + b) % per] for d in range(16)]
        grad_keys[128 * b : 128 * b + 128, :] = jnp.concatenate(columns, 0).T

    for copy in crossing + direct + gathered + forward + [share_first]:
        copy.wait_send()

    @pl.when(core == 0)
    def _():
        terms_all(0, 1, alone_sem).wait_send()
        terms_all(1, 2, terms_sem).wait_send()
        for copy in part_even:
            copy.wait_send()

    @pl.when(core == 1)
    def _():
        share_second.wait_send()
        terms_all(3, 1, alone_sem).wait_send()
        terms_all(2, 1, terms_sem).wait_send()
        part_odd.wait_send()

    all_of(ask_out, ask_in, ask_sem).wait_send()
    all_of(mass_out, mass_in, mass_sem).wait_send()
    all_of(back_out, back_in, back_sem).wait_send()
    all_of(final, final, final_sem).wait_send()


def solution(mesh):
    ns, nh = mesh.shape["seq"], mesh.shape["head"]

    def shards(
        main_query,
        latent,
        main_outside,
        index_query,
        index_weights,
        index_keys,
        index_outside,
        query_pos,
        key_pos,
    ):
        q = main_query.shape[0]
        kb = latent.shape[0]
        window = STEPS * kb
        per = 16 * (kb // 128) // nh
        vmem = pl.BlockSpec(memory_space=pltpu.VMEM)
        whole = pl.BlockSpec(memory_space=pltpu.MemorySpace.HBM)
        dma = pltpu.SemaphoreType.DMA
        grad_query, grad_weight, grad_keys = pl.pallas_call(
            functools.partial(kernel, ns, nh),
            out_shape=(
                jax.ShapeDtypeStruct((q, 2 * IDIM), BF16),
                jax.ShapeDtypeStruct((2, q), F32),
                jax.ShapeDtypeStruct((kb, IDIM), F32),
            ),
            in_specs=[whole] * 9,
            out_specs=(vmem, vmem, vmem),
            scratch_shapes=[
                pltpu.VMEM((4, q), F32),
                pltpu.VMEM((2, q), F32),
                pltpu.VMEM((1, q), F32),
                pltpu.VMEM((1, q), jnp.int32),
                pltpu.VMEM((1, kb), jnp.int32),
                pltpu.VMEM((128, q), F32),
                pltpu.VMEM((q, 128), F32),
                pltpu.VMEM((1, window), F32),
                pltpu.VMEM((2, 2 * q, WIDE), BF16),
                pltpu.VMEM((STEPS, WIDE + PAD, kb), BF16),
                pltpu.VMEM((STEPS, kb, IDIM), BF16),
                pltpu.VMEM((q, 2 * IDIM), BF16),
                pltpu.VMEM((q, 2 * IDIM), F32),
                pltpu.VMEM((2, 2 * q, window), F32),
                pltpu.VMEM((2, 2 * q, 128), F32),
                pltpu.VMEM((2, 2 * q, 128), F32),
                pltpu.VMEM((8, window), F32),
                pltpu.VMEM((2, 8, window), F32),
                pltpu.VMEM((nh, 16, 128), BF16),
                pltpu.VMEM((nh, 16, 128), BF16),
                pltpu.VMEM((nh, 16, window // 4), BF16),
                pltpu.VMEM((nh, 16, window // 4), BF16),
                pltpu.VMEM((8 * nh, 128), F32),
                pltpu.VMEM((8 * nh, 128), F32),
                pltpu.VMEM((8 * nh, window), F32),
                pltpu.VMEM((8 * nh, window), BF16),
                pltpu.VMEM((8 * nh, window), BF16),
                pltpu.VMEM((STEPS, nh, per, 8, 128), F32),
                pltpu.VMEM((STEPS, nh, per, 8, 128), F32),
                pltpu.VMEM((2, nh, per, 8, 128), F32),
                pltpu.VMEM((nh, 16, 128), BF16),
                pltpu.VMEM((nh, 16, 128), BF16),
                pltpu.VMEM((STEPS, per, 8, 128), F32),
                pltpu.VMEM((2, per, 8, 128), F32),
                pltpu.VMEM((nh, per, 8, 128), F32),
                pltpu.VMEM((q, 128), F32),
                dma((5,)),
                dma((7,)),
                dma((3,)),
                dma((3,)),
                dma((2,)),
                dma((2,)),
                dma((3,)),
                dma((3,)),
                dma((3,)),
                dma((3,)),
                dma((2,)),
                dma((2,)),
                dma((2,)),
                dma((2,)),
                dma((2,)),
                dma((2,)),
                dma((2,)),
                dma((STEPS - 1,)),
                dma((2,)),
                dma((2,)),
            ],
            compiler_params=pltpu.CompilerParams(
                collective_id=0, has_side_effects=True, vmem_limit_bytes=48 << 20
            ),
        )(
            *(
                pltpu.with_memory_space_constraint(x, pltpu.MemorySpace.HBM)
                for x in (
                    main_query,
                    latent.T,
                    main_outside.T,
                    index_query,
                    index_weights.T,
                    index_keys,
                    index_outside.reshape(1, q),
                    query_pos.reshape(1, q),
                    key_pos.reshape(1, kb),
                )
            )
        )
        return grad_query, grad_weight.T, grad_keys

    in_specs = (
        P("seq", "head"),
        P("seq", None),
        P("seq", "head"),
        P("seq", "head"),
        P("seq", "head"),
        P("seq", None),
        P("seq"),
        P("seq"),
        P("seq"),
    )
    out_specs = (P("seq", "head"), P("seq", "head"), P("seq", None))
    return jax.shard_map(shards, mesh=mesh, in_specs=in_specs, out_specs=out_specs, check_vma=False)
```

```python
import functools

import jax
import jax.numpy as jnp
from jax import lax
from jax.experimental import pallas as pl
from jax.experimental.pallas import tpu as pltpu
from jax.sharding import PartitionSpec as P

MESH = pl.DeviceIdType.MESH
STEPS = 4
IDIM = 128
WIDTH = 576
PAD = 64
WIDE = WIDTH + PAD
X_RUN = 4
X_ROWS = 320
Z_ROWS = WIDTH - X_ROWS
NEGATIVE = -1e30
ABSENT = 1e9
SCORE_SCALE = 192.0 ** (-0.5)
FACTOR = IDIM ** (-0.5)
F32 = jnp.float32
BF16 = jnp.bfloat16


def dot(a, b, dims):
    return lax.dot_general(a, b, (dims, ((), ())), preferred_element_type=F32)


def swap(x):
    return pltpu.roll(x, 4, 0)


def split_pair(a, b, low):
    return jnp.where(low, a, swap(b)), jnp.where(low, swap(a), b)


def high_part(x):
    return x.astype(BF16).astype(F32)


def kernel(
    ns,
    nh,
    main_query,
    latent,
    far_outside,
    index_query,
    far_weights,
    index_keys,
    far_limit,
    far_query_pos,
    far_key_pos,
    grad_query,
    grad_weight,
    grad_keys,
    outside,
    index_weights,
    index_outside,
    query_pos,
    key_pos,
    rows,
    cols,
    place,
    queries,
    lat,
    keys,
    narrow_query,
    wide_query,
    scores,
    peaks,
    sums,
    index_score,
    dscores,
    ask_out,
    ask_in,
    mass_out,
    mass_in,
    near_query,
    near_weight,
    act,
    upper,
    lower,
    terms_out,
    terms_in,
    shared,
    back_out,
    back_in,
    part_out,
    part_in,
    final,
    weight_grad,
    small_sem,
    local_sem,
    cross_send,
    cross_recv,
    direct_send,
    direct_recv,
    gather_send,
    gather_recv,
    forward_send,
    forward_recv,
    ask_sem,
    mass_sem,
    terms_sem,
    alone_sem,
    back_sem,
    shared_send,
    shared_recv,
    part_send,
    part_recv,
    final_sem,
):
    q_rows = index_query.shape[0]
    kb = key_pos.shape[1]
    window = STEPS * kb
    half = window // 2
    chunks = q_rows // 8
    blocks = kb // 128
    tiles = 16 * blocks
    per = tiles // nh
    head = lax.axis_index("head")
    seq = lax.axis_index("seq")

    local = []
    for parity in range(2):
        for i in range(2):
            start = (2 * i + parity) * WIDTH - parity * PAD
            local.append(
                pltpu.make_async_copy(
                    main_query.at[:, pl.ds(start, WIDE)],
                    queries.at[parity, pl.ds(i * q_rows, q_rows), :],
                    local_sem.at[2 * parity + i],
                )
            )
    local.append(
        pltpu.make_async_copy(latent, lat.at[STEPS - 1, pl.ds(PAD, WIDTH), :], local_sem.at[4])
    )
    local.append(pltpu.make_async_copy(index_keys, keys.at[STEPS - 1], local_sem.at[5]))
    local.append(pltpu.make_async_copy(index_query, narrow_query, local_sem.at[6]))
    small = [
        pltpu.make_async_copy(source, target, small_sem.at[i])
        for i, (source, target) in enumerate(
            (
                (far_outside, outside),
                (far_weights, index_weights),
                (far_limit, index_outside),
                (far_query_pos, query_pos),
                (far_key_pos, key_pos),
            )
        )
    ]
    for copy in small + local[6:] + local[:6]:
        copy.start()

    barrier = pltpu.get_barrier_semaphore()

    def greet(r, carry):
        pl.semaphore_signal(
            barrier, inc=1, device_id={"head": lax.rem(head + r, nh)}, device_id_type=MESH
        )
        return carry

    for distance in range(1, STEPS):
        for other in (seq + distance, seq + ns - distance):
            pl.semaphore_signal(
                barrier, inc=1, device_id={"seq": lax.rem(other, ns)}, device_id_type=MESH
            )
    lax.fori_loop(1, nh, greet, 0)

    pl.semaphore_wait(barrier, nh - 1 + 2 * (STEPS - 1))

    core = lax.rem(seq, 2)
    early, late = 2 * core, 2 - 2 * core
    ring, run = head // X_RUN, lax.rem(head, X_RUN)
    rings = nh // X_RUN
    run_rows, ring_rows, key_rows = X_ROWS // X_RUN, Z_ROWS // rings, kb // rings
    run_at = pl.multiple_of(run_rows * run, 16)
    ring_at = pl.multiple_of(X_ROWS + ring_rows * ring, 16)
    key_at = pl.multiple_of(key_rows * ring, 16)

    def lat_rows(slot, start, size):
        return lat.at[slot, pl.ds(pl.multiple_of(PAD + start, 16), size), :]

    def key_part(slot, start, size):
        return keys.at[slot, pl.ds(start, size), :]

    def to_seq(source, target, send, recv, i, other):
        return pltpu.make_async_remote_copy(
            src_ref=source,
            dst_ref=target,
            send_sem=send.at[i],
            recv_sem=recv.at[i],
            device_id={"seq": other},
            device_id_type=MESH,
        )

    two = lax.rem(seq + 2, ns)
    sibling = seq + 1 - 2 * core
    crossing = [
        to_seq(
            index_keys.at[pl.ds(key_at, key_rows), :],
            key_part(1, key_at, key_rows),
            cross_send, cross_recv, 0, two,
        ),
        to_seq(
            latent.at[pl.ds(ring_at, ring_rows), :],
            lat_rows(1, ring_at, ring_rows),
            cross_send, cross_recv, 1, two,
        ),
        to_seq(
            latent.at[pl.ds(run_at, run_rows), :],
            lat_rows(1, run_at, run_rows),
            cross_send, cross_recv, 2, two,
        ),
    ]
    onward = lax.rem(seq + 1 + 2 * core, ns)
    direct = [
        to_seq(index_keys, keys.at[late], direct_send, direct_recv, 0, onward),
        to_seq(latent, lat_rows(late, 0, WIDTH), direct_send, direct_recv, 1, onward),
    ]
    for copy in crossing[::-1] + direct[::-1]:
        copy.start()

    def exchange(source, target, sems, peer, slot):
        return pltpu.make_async_remote_copy(
            src_ref=source,
            dst_ref=target,
            send_sem=sems.at[0],
            recv_sem=sems.at[1],
            device_id={"head": peer},
            device_id_type=MESH,
        )

    def all_of(source, target, sems):
        return exchange(
            source.at[pl.ds(0, nh - 1)], target.at[pl.ds(0, nh - 1)], sems, lax.rem(head + 1, nh), 0
        )

    low = lax.broadcasted_iota(jnp.int32, (8, 128), 0) < 4
    lane = lax.broadcasted_iota(jnp.int32, (8, 128), 1)
    for copy in small:
        copy.wait()
    rows[...] = jnp.zeros_like(rows)
    rows[0:4, :] = outside[...]
    rows[4:6, :] = index_weights[...]
    rows[6:7, :] = query_pos[...].astype(F32)
    rows[7:8, :] = index_outside[...]
    cols[...] = rows[...].T
    for k in range(STEPS):
        here = jnp.where(seq >= STEPS - 1 - k, 0.0, ABSENT)
        own = key_pos[...].astype(F32) if k == STEPS - 1 else jnp.zeros((1, kb), F32)
        place[:, k * kb : (k + 1) * kb] = own + here
        lat[k, 0:PAD, :] = jnp.zeros((PAD, kb), BF16)
        lat[k, PAD + WIDTH : PAD + WIDTH + PAD, :] = jnp.zeros((PAD, kb), BF16)
    wide_lane = lax.broadcasted_iota(jnp.int32, (q_rows, 128), 1)
    for parity in range(2):
        for i in range(2):
            at = slice(i * q_rows, (i + 1) * q_rows)
            h = 2 * i + parity
            peaks[parity, at, :] = jnp.where(wide_lane == STEPS, cols[:, h : h + 1], NEGATIVE)
            sums[parity, at, :] = jnp.where(wide_lane == STEPS, 1.0, 0.0)
    local[6].wait()
    wide_query[...] = narrow_query[...].astype(F32)

    def ask(c, carry):
        at = pl.ds(pl.multiple_of(8 * c, 8), 8)
        values = wide_query[at, :]
        column = cols[at, :]
        first = jnp.broadcast_to(column[:, 4:5], (8, 128))
        second = jnp.broadcast_to(column[:, 5:6], (8, 128))
        pair = split_pair(values[:, :IDIM], values[:, IDIM:], low)
        weights = split_pair(first, second, low)
        for i in range(2):
            weight = weights[i]
            top = high_part(weight)
            mid = high_part(weight - top)
            end = weight - top - mid
            packed = jnp.where(lane == 0, top, jnp.where(lane == 1, mid, end))
            ask_out[2 * c + i] = jnp.concatenate([pair[i], packed], 0).astype(BF16)
        return carry

    lax.fori_loop(0, chunks, ask, 0)

    def send_ask(r, carry):
        peer = lax.rem(head + r, nh)
        exchange(ask_out.at[peer], ask_in.at[nh - 1 - r], ask_sem, peer, 0).start()
        return carry

    lax.fori_loop(1, nh, send_ask, 0)
    ask_in[nh - 1] = ask_out[head]

    def score_block(k):
        at = pl.ds(pl.multiple_of(k * kb, 128), kb)
        visible = place[:, at] <= cols[:, 6:7]
        for parity in range(2):
            table = lat[k, PAD * (1 - parity) : PAD * (1 - parity) + WIDE, :]
            x = dot(queries[parity], table, ((1,), (0,))) * SCORE_SCALE
            for i in range(2):
                own = slice(i * q_rows, (i + 1) * q_rows)
                masked = jnp.where(visible, x[own, :], NEGATIVE)
                peak = jnp.max(masked, axis=1, keepdims=True)
                e = jnp.exp(masked - peak)
                scores[parity, own, at] = e
                total = jnp.sum(e, axis=1, keepdims=True)
                peaks[parity, own, :] = jnp.where(wide_lane == k, peak, peaks[parity, own, :])
                sums[parity, own, :] = jnp.where(wide_lane == k, total, sums[parity, own, :])

    def act_block(k, asked):
        at = pl.ds(pl.multiple_of(k * kb, 128), kb)
        a = dot(asked, keys[k], ((1,), (1,))) * FACTOR
        act[:, at] = a
        weight = near_weight[...]
        weighed = jnp.concatenate([weight] * blocks, 1) * jnp.maximum(a, 0.0)
        index_score[:, at] = jnp.sum(weighed.reshape(nh, 8, kb), axis=0)

    def to_head(part, i, peer):
        return pltpu.make_async_remote_copy(
            src_ref=part,
            dst_ref=part,
            send_sem=gather_send.at[i],
            recv_sem=gather_recv.at[i],
            device_id={"head": peer},
            device_id_type=MESH,
        )

    for copy in local[:6]:
        copy.wait()
    score_block(STEPS - 1)
    def push_run(r, carry):
        peer = ring * X_RUN + lax.rem(run + r, X_RUN)
        to_head(lat_rows(1, run_at, run_rows), 2, peer).start()
        return carry

    def push_ring(r, carry):
        r = rings - r
        r = (r + 1) // 2 + lax.rem(r + 1, 2) * (rings - r)
        peer = lax.rem(head + r * X_RUN, nh)
        to_head(lat_rows(1, ring_at, ring_rows), 1, peer).start()
        return carry

    def push_keys(r, carry):
        peer = lax.rem(head + r * X_RUN, nh)
        to_head(key_part(1, key_at, key_rows), 0, peer).start()
        return carry

    crossing[2].wait_recv()
    lax.fori_loop(1, X_RUN, push_run, 0)
    crossing[1].wait_recv()
    lax.fori_loop(1, rings, push_ring, 0)
    crossing[0].wait_recv()
    lax.fori_loop(1, rings, push_keys, 0)
    gathered = [
        to_head(key_part(1, 0, key_rows * (rings - 1)), 0, head),
        to_head(lat_rows(1, 0, ring_rows * (rings - 1)), 1, head),
        to_head(lat_rows(1, 0, run_rows * (X_RUN - 1)), 2, head),
    ]
    forward = [
        to_seq(keys.at[1], keys.at[early], forward_send, forward_recv, 0, sibling),
        to_seq(
            lat_rows(1, X_ROWS, Z_ROWS),
            lat_rows(early, X_ROWS, Z_ROWS),
            forward_send, forward_recv, 1, sibling,
        ),
        to_seq(
            lat_rows(1, 0, X_ROWS),
            lat_rows(early, 0, X_ROWS),
            forward_send, forward_recv, 2, sibling,
        ),
    ]
    for copy in direct:
        copy.wait_recv()
    score_block(early)
    for i in (2, 1):
        gathered[i].wait_recv()
        forward[i].start()
    score_block(1)
    gathered[0].wait_recv()
    forward[0].start()


    forward[1].wait_recv()
    forward[2].wait_recv()
    score_block(late)

    for parity in range(2):
        peak = peaks[parity]
        share = jnp.exp(peak - jnp.max(peak, axis=1, keepdims=True))
        total = jnp.sum(share * sums[parity], axis=1, keepdims=True)
        peaks[parity] = share * (1.0 / total)

    def soften(step, carry):
        c = lax.rem(step + head // 2 + 1, chunks)
        parts = []
        for k in range(STEPS):
            part = jnp.zeros((8, kb), F32)
            for parity in range(2):
                for i in range(2):
                    own = pl.ds(pl.multiple_of(i * q_rows + 8 * c, 8), 8)
                    part = part + (
                        scores[parity, own, k * kb : (k + 1) * kb] * peaks[parity, own, k : k + 1]
                    )
            parts.append(part)
        mass = jnp.concatenate(parts, 1)
        halves = split_pair(
            mass[:, :half], mass[:, half:], lax.broadcasted_iota(jnp.int32, (8, half), 0) < 4
        )
        for i in range(2):
            peer = 2 * c + i
            mass_out[peer] = jnp.concatenate(
                [halves[i][:, : half // 2], halves[i][:, half // 2 :]], 0
            ).astype(BF16)

            @pl.when(peer != head)
            def _():
                r = lax.rem(peer + nh - head, nh)
                exchange(mass_out.at[peer], mass_in.at[nh - 1 - r], mass_sem, peer, 0).start()

        return carry

    lax.fori_loop(0, chunks, soften, 0)
    mass_in[nh - 1] = mass_out[head]

    all_of(ask_out, ask_in, ask_sem).wait_recv()

    both = ask_in[...].astype(F32)
    near_query[...] = both[:, 0:8, :].reshape(8 * nh, 128)
    packed = both[:, 8:16, :].reshape(8 * nh, 128)
    weight = packed[:, 0:1] + (packed[:, 1:2] + packed[:, 2:3])
    near_weight[...] = jnp.broadcast_to(weight, (8 * nh, 128))
    asked = near_query[...].astype(BF16)
    act_block(STEPS - 1, asked)
    act_block(early, asked)
    act_block(1, asked)
    forward[0].wait_recv()
    act_block(late, asked)

    score = index_score[...]
    score = score + swap(score)
    odd = lax.rem(head, 2)
    column = cols[pl.ds(pl.multiple_of(8 * (head // 2), 8), 8), :]
    pick = (lax.broadcasted_iota(jnp.int32, (8, 128), 0) // 4) == odd
    column = jnp.where(pick, column, swap(column))
    visible = place[...] <= column[:, 6:7]
    masked = jnp.where(visible, score, NEGATIVE)
    limit = column[:, 7:8]
    top = jnp.maximum(jnp.max(masked, axis=1, keepdims=True), limit)
    e = jnp.exp(masked - top)
    total = jnp.sum(e, axis=1, keepdims=True) + jnp.exp(limit - top)
    predicted = e * (1.0 / total)
    weighted = near_weight[...] * near_query[...]
    turned = weighted.T
    turned_high = turned.astype(BF16)
    turned_low = (turned - turned_high.astype(F32)).astype(BF16)

    all_of(mass_out, mass_in, mass_sem).wait_recv()
    mass = mass_in[0].astype(F32)
    for g in range(1, nh):
        mass = mass + mass_in[g].astype(F32)
    mass = jnp.concatenate([mass[0:8, :], mass[8:16, :]], 1)
    low_half = lax.broadcasted_iota(jnp.int32, (8, half), 0) < 4
    turned_mass = swap(mass)
    mass = jnp.concatenate(
        [jnp.where(low_half, mass, turned_mass), jnp.where(low_half, turned_mass, mass)], 1
    )
    target = mass * (1.0 / jnp.sum(mass, axis=1, keepdims=True))
    dscore = (predicted - target) * float(window)
    d_high = high_part(dscore)
    dscores[0] = d_high
    dscores[1] = dscore - d_high

    def term_block(k):
        at = pl.ds(pl.multiple_of(k * kb, 128), kb)
        on = act[:, at].reshape(nh, 8, kb) > 0.0
        gated = []
        for i in range(2):
            chosen = jnp.where(on, dscores[i, :, at][None], 0.0)
            gated.append(chosen.reshape(8 * nh, kb).astype(BF16))
        upper[:, at] = gated[0]
        lower[:, at] = gated[1]
        terms = dot(turned_high, gated[0], ((1,), (0,)))
        terms = terms + dot(turned_low, gated[0], ((1,), (0,)))
        terms = terms + dot(turned_high, gated[1], ((1,), (0,)))
        terms = terms * FACTOR
        for tile in range(tiles):
            d, b = tile // blocks, tile % blocks
            terms_out[k, tile // per, tile % per] = terms[
                8 * d : 8 * d + 8, 128 * b : 128 * b + 128
            ]

    def terms_to(first, count, peer, slot, sems):
        return exchange(
            terms_out.at[pl.ds(first, count), peer],
            terms_in.at[pl.ds(first, count), slot],
            sems, peer, 0,
        )

    def terms_all(first, count, sems):
        return exchange(
            terms_out.at[pl.ds(first, count), pl.ds(0, nh - 1)],
            terms_in.at[pl.ds(first, count), pl.ds(0, nh - 1)],
            sems, lax.rem(head + 1, nh), 0,
        )

    def send_terms(first, count, sems):
        def send(r, carry):
            terms_to(first, count, lax.rem(head + r, nh), nh - 1 - r, sems).start()
            return carry

        lax.fori_loop(1, nh, send, 0)

    term_block(3 - 3 * core)
    share_first = to_seq(
        terms_out.at[3 - 3 * core], shared.at[0], shared_send, shared_recv, 0, sibling
    )
    share_second = to_seq(terms_out.at[1], shared.at[1], shared_send, shared_recv, 1, sibling)
    share_first.start()
    term_block(core)

    @pl.when(core == 1)
    def _():
        share_second.start()

    term_block(1 + 2 * core)
    send_terms(3 * core, 1, alone_sem)
    term_block(2)
    share_first.wait_recv()

    @pl.when(core == 0)
    def _():
        share_second.wait_recv()
        terms_out[1] = terms_out[1] + shared[0]
        terms_out[2] = terms_out[2] + shared[1]
        send_terms(1, 2, terms_sem)

    @pl.when(core == 1)
    def _():
        terms_out[2] = terms_out[2] + shared[0]
        send_terms(2, 1, terms_sem)

    all_keys = keys[...].reshape(window, IDIM)
    near_grad = dot(upper[...], all_keys, ((1,), (0,))) + dot(lower[...], all_keys, ((1,), (0,)))
    near_grad = near_grad * FACTOR * near_weight[...]

    share = jnp.zeros((8 * nh, 1), F32)
    for k in range(STEPS):
        at = slice(k * kb, (k + 1) * kb)
        rectified = jnp.maximum(act[:, at], 0.0).reshape(nh, 8, kb)
        product = (rectified * dscore[:, at][None]).reshape(8 * nh, kb)
        share = share + jnp.sum(product, axis=1, keepdims=True)
    tall_lane = lax.broadcasted_iota(jnp.int32, (8 * nh, 128), 1)
    top = high_part(share)
    mid = high_part(share - top)
    packed = jnp.where(tall_lane == 0, top, jnp.where(tall_lane == 1, mid, share - top - mid))
    back_out[...] = jnp.concatenate(
        [near_grad.reshape(nh, 8, 128), packed.reshape(nh, 8, 128)], 1
    ).astype(BF16)

    def sum_terms(k):
        total = terms_out[k, head]
        for g in range(nh - 1):
            total = total + terms_in[k, g]
        part_out[k] = total

    behind = lax.rem(seq + ns - 2, ns)

    def part(k, slot, other):
        return pltpu.make_async_remote_copy(
            src_ref=part_out.at[k],
            dst_ref=part_in.at[slot],
            send_sem=part_send.at[k],
            recv_sem=part_recv.at[slot],
            device_id={"seq": other},
            device_id_type=MESH,
        )

    part_even = [
        part(1, 1, behind),
        part(2, 0, lax.rem(seq + ns - 1, ns)),
        part(0, 1, lax.rem(seq + ns - 3, ns)),
    ]
    part_odd = part(2, 0, sibling)

    @pl.when(core == 0)
    def _():
        terms_all(0, 1, alone_sem).wait_recv()
        sum_terms(0)
        part_even[2].start()
        terms_all(1, 2, terms_sem).wait_recv()
        for k in (1, 2):
            sum_terms(k)
            part_even[k - 1].start()

    @pl.when(core == 1)
    def _():
        terms_all(3, 1, alone_sem).wait_recv()
        sum_terms(3)
        terms_all(2, 1, terms_sem).wait_recv()
        sum_terms(2)
        part_odd.start()

    def send_back(r, carry):
        peer = lax.rem(head + r, nh)
        exchange(back_out.at[r - 1], back_in.at[head], back_sem, peer, 0).start()
        return carry

    lax.fori_loop(1, nh, send_back, 0)
    back_in[head] = back_out[nh - 1]

    part(1, 0, behind).wait_recv()
    part(1, 1, behind).wait_recv()
    mine = jnp.where(core == 1, part_out[3], 0.0) + part_in[0] + part_in[1]
    final[head] = mine

    def send_final(r, carry):
        peer = lax.rem(head + r, nh)
        exchange(final.at[head], final.at[head], final_sem, peer, 0).start()
        return carry

    lax.fori_loop(1, nh, send_final, 0)

    all_of(back_out, back_in, back_sem).wait_recv()

    def unpack_back(c, carry):
        at = pl.ds(pl.multiple_of(8 * c, 8), 8)
        one = back_in[2 * c].astype(F32)
        two = back_in[2 * c + 1].astype(F32)
        first, second = split_pair(one[0:8, :], two[0:8, :], low)
        wide_query[at, 0:IDIM] = first
        wide_query[at, IDIM : 2 * IDIM] = second
        shares = []
        for packed in (one[8:16, :], two[8:16, :]):
            share = packed[:, 0:1] + (packed[:, 1:2] + packed[:, 2:3])
            shares.append(jnp.broadcast_to(share, (8, 128)))
        first, second = split_pair(shares[0], shares[1], low)
        weight_grad[at, :] = jnp.where(lane == 0, first, second)
        return carry

    lax.fori_loop(0, chunks, unpack_back, 0)
    grad_query[...] = wide_query[...].astype(BF16)
    grad_weight[...] = weight_grad[...].T[0:2, :]

    all_of(final, final, final_sem).wait_recv()
    for b in range(blocks):
        columns = [final[(d * blocks + b) // per, (d * blocks + b) % per] for d in range(16)]
        grad_keys[128 * b : 128 * b + 128, :] = jnp.concatenate(columns, 0).T

    for copy in crossing + direct + gathered + forward + [share_first]:
        copy.wait_send()

    @pl.when(core == 0)
    def _():
        terms_all(0, 1, alone_sem).wait_send()
        terms_all(1, 2, terms_sem).wait_send()
        for copy in part_even:
            copy.wait_send()

    @pl.when(core == 1)
    def _():
        share_second.wait_send()
        terms_all(3, 1, alone_sem).wait_send()
        terms_all(2, 1, terms_sem).wait_send()
        part_odd.wait_send()

    all_of(ask_out, ask_in, ask_sem).wait_send()
    all_of(mass_out, mass_in, mass_sem).wait_send()
    all_of(back_out, back_in, back_sem).wait_send()
    all_of(final, final, final_sem).wait_send()


def solution(mesh):
    ns, nh = mesh.shape["seq"], mesh.shape["head"]

    def shards(
        main_query,
        latent,
        main_outside,
        index_query,
        index_weights,
        index_keys,
        index_outside,
        query_pos,
        key_pos,
    ):
        q = main_query.shape[0]
        kb = latent.shape[0]
        window = STEPS * kb
        per = 16 * (kb // 128) // nh
        vmem = pl.BlockSpec(memory_space=pltpu.VMEM)
        whole = pl.BlockSpec(memory_space=pltpu.MemorySpace.HBM)
        dma = pltpu.SemaphoreType.DMA
        grad_query, grad_weight, grad_keys = pl.pallas_call(
            functools.partial(kernel, ns, nh),
            out_shape=(
                jax.ShapeDtypeStruct((q, 2 * IDIM), BF16),
                jax.ShapeDtypeStruct((2, q), F32),
                jax.ShapeDtypeStruct((kb, IDIM), F32),
            ),
            in_specs=[whole] * 9,
            out_specs=(vmem, vmem, vmem),
            scratch_shapes=[
                pltpu.VMEM((4, q), F32),
                pltpu.VMEM((2, q), F32),
                pltpu.VMEM((1, q), F32),
                pltpu.VMEM((1, q), jnp.int32),
                pltpu.VMEM((1, kb), jnp.int32),
                pltpu.VMEM((128, q), F32),
                pltpu.VMEM((q, 128), F32),
                pltpu.VMEM((1, window), F32),
                pltpu.VMEM((2, 2 * q, WIDE), BF16),
                pltpu.VMEM((STEPS, WIDE + PAD, kb), BF16),
                pltpu.VMEM((STEPS, kb, IDIM), BF16),
                pltpu.VMEM((q, 2 * IDIM), BF16),
                pltpu.VMEM((q, 2 * IDIM), F32),
                pltpu.VMEM((2, 2 * q, window), F32),
                pltpu.VMEM((2, 2 * q, 128), F32),
                pltpu.VMEM((2, 2 * q, 128), F32),
                pltpu.VMEM((8, window), F32),
                pltpu.VMEM((2, 8, window), F32),
                pltpu.VMEM((nh, 16, 128), BF16),
                pltpu.VMEM((nh, 16, 128), BF16),
                pltpu.VMEM((nh, 16, window // 4), BF16),
                pltpu.VMEM((nh, 16, window // 4), BF16),
                pltpu.VMEM((8 * nh, 128), F32),
                pltpu.VMEM((8 * nh, 128), F32),
                pltpu.VMEM((8 * nh, window), F32),
                pltpu.VMEM((8 * nh, window), BF16),
                pltpu.VMEM((8 * nh, window), BF16),
                pltpu.VMEM((STEPS, nh, per, 8, 128), F32),
                pltpu.VMEM((STEPS, nh, per, 8, 128), F32),
                pltpu.VMEM((2, nh, per, 8, 128), F32),
                pltpu.VMEM((nh, 16, 128), BF16),
                pltpu.VMEM((nh, 16, 128), BF16),
                pltpu.VMEM((STEPS, per, 8, 128), F32),
                pltpu.VMEM((2, per, 8, 128), F32),
                pltpu.VMEM((nh, per, 8, 128), F32),
                pltpu.VMEM((q, 128), F32),
                dma((5,)),
                dma((7,)),
                dma((3,)),
                dma((3,)),
                dma((2,)),
                dma((2,)),
                dma((3,)),
                dma((3,)),
                dma((3,)),
                dma((3,)),
                dma((2,)),
                dma((2,)),
                dma((2,)),
                dma((2,)),
                dma((2,)),
                dma((2,)),
                dma((2,)),
                dma((STEPS - 1,)),
                dma((2,)),
                dma((2,)),
            ],
            compiler_params=pltpu.CompilerParams(
                collective_id=0, has_side_effects=True, vmem_limit_bytes=48 << 20
            ),
        )(
            *(
                pltpu.with_memory_space_constraint(x, pltpu.MemorySpace.HBM)
                for x in (
                    main_query,
                    latent.T,
                    main_outside.T,
                    index_query,
                    index_weights.T,
                    index_keys,
                    index_outside.reshape(1, q),
                    query_pos.reshape(1, q),
                    key_pos.reshape(1, kb),
                )
            )
        )
        return grad_query, grad_weight.T, grad_keys

    in_specs = (
        P("seq", "head"),
        P("seq", None),
        P("seq", "head"),
        P("seq", "head"),
        P("seq", "head"),
        P("seq", None),
        P("seq"),
        P("seq"),
        P("seq"),
    )
    out_specs = (P("seq", "head"), P("seq", "head"), P("seq", None))
    return jax.shard_map(shards, mesh=mesh, in_specs=in_specs, out_specs=out_specs, check_vma=False)
```
